256 devices in a mesh: dp: 2 (over core), tensor: 8 (over z), expert: 16 (over y, x).
Axes of the slice: x: 4, y: 4, z: 8, core: 2. Of those that a mesh axis runs over, the one named last changes fastest.
Arguments:
- attn_heads: bfloat16 [32, 64, 4096], P(('dp', 'expert'), None, 'tensor'), may hold values from -6 to 6
- out_proj: bfloat16 [4096, 4096], P('tensor'), may hold values from -0.09375 to 0.09375
- residual: bfloat16 [32, 64, 4096], P(('dp', 'expert'), 'tensor'), may hold values from -6 to 6
- norm_gain: float32 [4096], replicated, may hold values from 0.25 to 1.75
- expert_ids: int32 [32, 64, 8], P(('dp', 'expert'), 'tensor'), may hold values from 0 to 15, all different within a row; in each aligned block of 8 rows (0 to 7, 8 to 15, ..., all dimensions but the last counted through in order) at most 6 rows name the same one
- weight_codes: int32 [32, 64, 8], P(('dp', 'expert'), 'tensor'), may hold values from 1 to 16
- w_gate: bfloat16 [16, 1536, 4096], P('expert', 'tensor'), may hold values from -0.09375 to 0.09375
- w_up: bfloat16 [16, 1536, 4096], P('expert', 'tensor'), may hold values from -0.09375 to 0.09375
- w_down: bfloat16 [16, 1536, 4096], P('expert', 'tensor'), may hold values from -0.625 to 0.625
Outputs:
- layer_out: bfloat16 [32, 64, 4096], P(('dp', 'expert'), 'tensor')
The draws below stay inside these ranges and needn't reach their ends.
Inputs may be any that keep to these rules, and one draw needn't show every extreme that they name: `expert_ids`: each token names 8 different experts. Among the 8 consecutive tokens of one device (aligned blocks of the flattened first two dimensions) no expert is named by more than 6 rows, and every draw has an expert named exactly 6 times in some device's rows.
All inputs are finite; a program needn't handle non-finite values.
Results may differ from the reference program's by a relative error of at most 0.022.
Values may be sent and summed in bfloat16 or wider, within the bound.
No kernel may reach another device: no remote copies, remote signals or barrier semaphores. Data moves between devices by JAX's collectives and lax.ppermute only.
A program may use at most 128 MiB of HBM per device.

```python
import math
import jax
import jax.numpy as jnp
import numpy as np
from jax import lax

D = 4096
FF = 1536
HD = 128
HQ = 32
EXPERTS = 16
TOP = 8
TOK_DEV = 8
CAP = 6
GROUP_TOK = 64
GROUPS = 32
N_TENSOR = 8


def with_ends(array, own_key, smallest, top_value):
    index_at = [jax.random.randint(jax.random.fold_in(own_key, axis), (), 0, length) for axis, length in enumerate(array.shape)]
    widest = array.shape.index(max(array.shape))
    neighbour = index_at[:widest] + [(index_at[widest] + 1) % array.shape[widest]] + index_at[widest + 1:]
    return array.at[tuple(index_at)].set(smallest).at[tuple(neighbour)].set(top_value)


def levels(own_key, extent, cuts, least, top_value):
    factor_of, own = 1.0, jax.random.fold_in(own_key, 6)
    for dim, blocks in cuts:
        heights = jnp.exp(jax.random.uniform(jax.random.fold_in(own, dim), (blocks,), jnp.float32, least / len(cuts), top_value / len(cuts)))
        factor_of = factor_of * jnp.repeat(heights, extent[dim] // blocks).reshape([-1 if axis == dim else 1 for axis in range(len(extent))])
    return factor_of


def routed_block(stream_key, own, number, rows, number_of, top, limit, lean):
    ranking = jax.random.permutation(stream_key, number_of)
    packed, usual = portions_of(number_of, rows * top, limit, lean, True), portions_of(number_of, rows * top, limit, lean, False)
    places = jnp.arange(number_of)

    def named(tallies, offset_by):
        used = int((tallies > 0).sum())
        fixed = max(1, used // 4)
        shifted = fixed + (places - fixed + offset_by * (used - fixed)) % max(1, number_of - fixed)
        return jnp.zeros((number_of,), jnp.int32).at[ranking[jnp.where(places < fixed, places, shifted)]].set(jnp.asarray(tallies, jnp.int32))

    tallies = jnp.where(number % 4 == 0, named(packed, number // 4), named(usual, number - number // 4 - 1))
    mixed = jax.random.permutation(jax.random.fold_in(own, 3), number_of)
    donor, receiver = mixed[0:number_of // 2 * 2:2], mixed[1:number_of // 2 * 2:2]
    margin = jnp.minimum(tallies[donor] - 1, limit - tallies[receiver]) // 2
    margin = jnp.where((donor == ranking[0]) | (receiver == ranking[0]) | (tallies[receiver] == 0), 0, jnp.maximum(margin, 0))
    shifted = jax.random.randint(jax.random.fold_in(own, 4), (number_of // 2,), 0, 1 << 20) % (margin + 1)
    tallies = tallies.at[donor].add(-shifted).at[receiver].add(shifted)
    items = jnp.searchsorted(jnp.cumsum(tallies), jnp.arange(rows * top), side="right").astype(jnp.int32)
    table = items.reshape(top, rows).T
    table = table[jax.random.permutation(jax.random.fold_in(own, 1), rows)]
    offset_by = jax.random.randint(jax.random.fold_in(own, 2), (rows, 1), 0, top)
    return jnp.take_along_axis(table, (jnp.arange(top)[None, :] + offset_by) % top, axis=1)


def portions_of(count, total, bound, slope, full):
    weights = [(1 << 20) // math.isqrt(grade ** slope) + 1 for grade in range(1, count + 1)]
    largest = bound if full else min(bound, max(-(-total // count), total * weights[0] // sum(weights)))
    least = 1 if total - largest >= count - 1 else 0
    counts, spare = [largest] + [least] * (count - 1), total - largest - least * (count - 1)
    while spare > 0:
        candidates = [i for i in range(1, count) if counts[i] < largest] or [i for i in range(1, count) if counts[i] < bound]
        pool, left = sum([weights[i] for i in candidates]), spare
        for i in candidates:
            extra = min(bound - counts[i], max(1, left * weights[i] // pool), spare)
            counts[i] = counts[i] + extra
            spare = spare - extra
    return np.array(counts)


def noise(stream_key, dims, deviation, reach, cuts=(), kind=jnp.bfloat16):
    values = deviation * jax.random.normal(stream_key, dims, jnp.float32)
    if cuts:
        values = values * levels(stream_key, dims, cuts, -0.22, 0.18)
    return jnp.clip(values, -reach, reach).astype(kind)


def setup_inputs(seed: int = 0) -> dict:
    keys = jax.random.split(jax.random.key(seed), 10)
    attn_heads = noise(keys[0], (GROUPS, GROUP_TOK, HQ * HD), 1.0, 6.0, ((0, 32), (2, 8)))
    out_proj = noise(keys[1], (HQ * HD, D), (HQ * HD) ** -0.5, 0.09375, ((0, 8),))
    residual = noise(keys[2], (GROUPS, GROUP_TOK, D), 1.0, 6.0, ((0, 32), (1, 8)))
    norm_gain = jnp.clip(1.0 + 0.15 * jax.random.normal(keys[3], (D,), jnp.float32), 0.25, 1.75)
    expert_ids_keys = jax.random.split(jax.random.fold_in(keys[4], 1), GROUPS * GROUP_TOK // TOK_DEV)
    expert_ids_turns = jax.random.permutation(jax.random.fold_in(keys[4], 3), GROUPS * GROUP_TOK // TOK_DEV)
    expert_ids = jax.vmap(lambda own, number: routed_block(jax.random.fold_in(keys[4], 2), own, number, TOK_DEV, EXPERTS, TOP, CAP, 2))(expert_ids_keys, expert_ids_turns).reshape((GROUPS, GROUP_TOK, TOP))
    weight_codes = with_ends(jax.random.randint(keys[5], (GROUPS, GROUP_TOK, TOP), 1, 17), jax.random.fold_in(keys[5], 1), 1, 16).astype(jnp.int32)
    w_gate = noise(keys[6], (EXPERTS, FF, D), D ** -0.5, 0.09375, ((0, 16), (1, 8)))
    w_up = noise(keys[7], (EXPERTS, FF, D), D ** -0.5, 0.09375, ((0, 16), (1, 8)))
    w_down = noise(keys[8], (EXPERTS, FF, D), (FF // 16) ** -0.5, 0.625, ((0, 16), (1, 8)))
    return dict(attn_heads=attn_heads, out_proj=out_proj, residual=residual, norm_gain=norm_gain, expert_ids=expert_ids, weight_codes=weight_codes, w_gate=w_gate, w_up=w_up, w_down=w_down)


def reference(attn_heads, out_proj, residual, norm_gain, expert_ids, weight_codes, w_gate, w_up, w_down):
    flat_heads = attn_heads.reshape(-1, HQ * HD)
    attn_sum = jnp.dot(flat_heads, out_proj, preferred_element_type=jnp.float32)
    hidden = residual.reshape(-1, D).astype(jnp.float32) + attn_sum
    mean_square = lax.optimization_barrier(jnp.mean(hidden * hidden, axis=-1, keepdims=True))
    normed = (hidden * lax.rsqrt(mean_square + 1e-06) * norm_gain).astype(jnp.bfloat16)
    route_ids = expert_ids.reshape(-1, TOP)
    code_values = weight_codes.reshape(-1, TOP).astype(jnp.float32)
    mixing = code_values / lax.optimization_barrier(jnp.sum(code_values, axis=-1, keepdims=True))
    slice_width = FF // N_TENSOR

    def one_expert(total_sum, expert_num):
        weight_expert = lax.optimization_barrier(jnp.sum(jnp.where(route_ids == expert_num, mixing, jnp.float32(0.0)), axis=-1))
        gate_value = jnp.dot(normed, w_gate[expert_num].T, preferred_element_type=jnp.float32)
        up_value = jnp.dot(normed, w_up[expert_num].T, preferred_element_type=jnp.float32)
        activated = (jax.nn.silu(gate_value) * up_value).astype(jnp.bfloat16)
        down_expert = w_down[expert_num]
        accumulated = jnp.zeros((normed.shape[0], D), jnp.float32)
        for block_num in range(N_TENSOR):
            partial_value = jnp.dot(activated[:, block_num * slice_width:(block_num + 1) * slice_width], down_expert[block_num * slice_width:(block_num + 1) * slice_width], preferred_element_type=jnp.float32).astype(jnp.bfloat16)
            partial_value = lax.optimization_barrier(partial_value)
            accumulated = accumulated + partial_value.astype(jnp.float32)
        expert_out = lax.optimization_barrier(accumulated.astype(jnp.bfloat16))
        return (total_sum + weight_expert[:, None] * expert_out.astype(jnp.float32), None)
    expert_mix, _ = lax.scan(one_expert, jnp.zeros(hidden.shape, jnp.float32), jnp.arange(EXPERTS, dtype=jnp.int32))
    layer_out = (hidden + expert_mix).astype(jnp.bfloat16)
    return layer_out.reshape(residual.shape)
```

```python
import jax
import jax.numpy as jnp
from jax import lax
from jax.sharding import PartitionSpec as P

EXPERTS = 16
TOP = 8
CAP = 6
EXTRA = 128


def normalize(hidden, norm_gain):
    mean_square = jnp.mean(hidden * hidden, axis=-1, keepdims=True)
    return (hidden * lax.rsqrt(mean_square + 1e-06) * norm_gain).astype(jnp.bfloat16)


def reduce_over_tensor(partial):
    count = lax.axis_size("tensor")
    parts = lax.all_to_all(
        partial.astype(jnp.bfloat16), "tensor", split_axis=0, concat_axis=0, tiled=True
    )
    parts = parts.reshape(count, partial.shape[0] // count, partial.shape[1])
    return jnp.sum(parts.astype(jnp.float32), axis=0)


def on_device(
    attn_heads, out_proj, residual, norm_gain, expert_ids, weight_codes, w_gate, w_up, w_down
):
    tensor_count = lax.axis_size("tensor")
    expert_count = lax.axis_size("expert")
    own_residual = residual[0]
    tok_own, model_width = own_residual.shape
    tokens = tok_own * tensor_count
    slots = CAP * tensor_count

    partial = jnp.dot(attn_heads[0], out_proj, preferred_element_type=jnp.float32)
    hidden = own_residual.astype(jnp.float32) + reduce_over_tensor(partial)
    normed = normalize(hidden, norm_gain)

    routes = jnp.concatenate([expert_ids[0], weight_codes[0]], axis=1).astype(jnp.bfloat16)
    routes = jnp.pad(routes, ((0, 0), (0, EXTRA - 2 * TOP)))
    group = lax.all_gather(
        jnp.concatenate([normed, routes], axis=1), "tensor", axis=0, tiled=True
    )
    group_normed = group[:, :model_width]
    ids = group[:, model_width : model_width + TOP].astype(jnp.int32)
    codes = group[:, model_width + TOP : model_width + 2 * TOP].astype(jnp.float32)

    names = ids[:, :, None] == jnp.arange(EXPERTS, dtype=jnp.int32)[None, None, :]
    table = jnp.sum(jnp.where(names, codes[:, :, None], 0.0), axis=1)
    routed = jnp.any(names, axis=1)
    earlier = jnp.tril(jnp.ones((tokens, tokens), jnp.float32), -1)
    place = jnp.dot(earlier, routed.astype(jnp.float32)).astype(jnp.int32)
    place = jnp.where(routed, place, -1)
    at_slot = place.T[:, None, :] == jnp.arange(slots, dtype=jnp.int32)[None, :, None]
    spread = at_slot.astype(jnp.bfloat16).reshape(EXPERTS * slots, tokens)
    outgoing = jnp.dot(spread, group_normed, preferred_element_type=jnp.float32)
    arrived = lax.all_to_all(
        outgoing.astype(jnp.bfloat16), "expert", split_axis=0, concat_axis=0, tiled=True
    )

    gate_value = jnp.einsum("rd,fd->rf", arrived, w_gate[0], preferred_element_type=jnp.float32)
    up_value = jnp.einsum("rd,fd->rf", arrived, w_up[0], preferred_element_type=jnp.float32)
    activated = (jax.nn.silu(gate_value) * up_value).astype(jnp.bfloat16)
    expert_part = jnp.dot(activated, w_down[0], preferred_element_type=jnp.float32)

    returned = lax.all_to_all(
        expert_part.astype(jnp.bfloat16), "expert", split_axis=0, concat_axis=0, tiled=True
    )
    weighted = jnp.where(at_slot, table.T[:, None, :], 0.0).astype(jnp.bfloat16)
    weighted = weighted.reshape(EXPERTS * slots, tokens)
    mixed = jnp.einsum("st,sd->td", weighted, returned, preferred_element_type=jnp.float32)
    mixed = mixed / jnp.sum(codes, axis=-1, keepdims=True)
    layer_out = (hidden + reduce_over_tensor(mixed)).astype(jnp.bfloat16)
    return layer_out[None]


def solution(mesh):
    return jax.shard_map(
        on_device,
        mesh=mesh,
        in_specs=(
            P(("dp", "expert"), None, "tensor"),
            P("tensor", None),
            P(("dp", "expert"), "tensor", None),
            P(),
            P(("dp", "expert"), "tensor", None),
            P(("dp", "expert"), "tensor", None),
            P("expert", "tensor", None),
            P("expert", "tensor", None),
            P("expert", "tensor", None),
        ),
        out_specs=P(("dp", "expert"), "tensor", None),
        check_vma=False,
    )
```

```python
import jax
import jax.numpy as jnp
from jax import lax
from jax.sharding import PartitionSpec as P

EXPERTS = 16
SIDE = 4
LANES = 128


def normalize(hidden, norm_gain):
    mean_square = jnp.mean(hidden * hidden, axis=-1, keepdims=True)
    return (hidden * lax.rsqrt(mean_square + 1e-06) * norm_gain).astype(jnp.bfloat16)


def together(*values):
    return lax.optimization_barrier(values)


def reduce_over_tensor(partial):
    count = lax.axis_size("tensor")
    parts = lax.all_to_all(
        partial.astype(jnp.bfloat16), "tensor", split_axis=0, concat_axis=0, tiled=True
    )
    parts = parts.reshape(count, partial.shape[0] // count, partial.shape[1])
    return jnp.sum(parts.astype(jnp.float32), axis=0)


def shift(value, axis, step):
    pairs = []
    for row in range(SIDE):
        for col in range(SIDE):
            if axis == "y":
                target = ((row + step) % SIDE) * SIDE + col
            else:
                target = row * SIDE + (col + step) % SIDE
            pairs.append((row * SIDE + col, target))
    return lax.ppermute(value, "expert", pairs)


def spread(first, first_axis, second, second_axis):
    half = first.shape[0] // 2
    near = together(
        shift(first, first_axis, 1),
        shift(first, first_axis, -1),
        shift(second, second_axis, 1),
        shift(second, second_axis, -1),
    )
    far = together(
        shift(near[0][:half], first_axis, 1),
        shift(near[1][half:], first_axis, -1),
        shift(near[2][:half], second_axis, 1),
        shift(near[3][half:], second_axis, -1),
    )
    return near, far


def add(*values):
    total = values[0].astype(jnp.float32)
    for value in values[1:]:
        total = total + value.astype(jnp.float32)
    return total


def collect(first, first_axis, second, second_axis):
    half = first[0].shape[0] // 2
    rp, rm, sp, sm = together(
        shift(first[2][:half], first_axis, 1),
        shift(first[2][half:], first_axis, -1),
        shift(second[2][:half], second_axis, 1),
        shift(second[2][half:], second_axis, -1),
    )

    def ahead(block, arrived):
        return jnp.concatenate([add(block[:half], arrived).astype(jnp.bfloat16), block[half:]])

    def behind(block, arrived):
        return jnp.concatenate([block[:half], add(block[half:], arrived).astype(jnp.bfloat16)])

    qp, qm, tp, tm = together(
        shift(ahead(first[3], rp), first_axis, 1),
        shift(behind(first[1], rm), first_axis, -1),
        shift(ahead(second[3], sp), second_axis, 1),
        shift(behind(second[1], sm), second_axis, -1),
    )
    return add(first[0], qp, qm), add(second[0], tp, tm)


def on_device(
    attn_heads, out_proj, residual, norm_gain, expert_ids, weight_codes, w_gate, w_up, w_down
):
    tensor_count = lax.axis_size("tensor")
    own_residual = residual[0]
    tok_own, model_width = own_residual.shape
    tokens = tok_own * tensor_count
    half = tokens // 2
    me = lax.axis_index("expert")
    my_row, my_col = me // SIDE, me % SIDE

    codes = weight_codes[0].astype(jnp.float32)
    mixing = codes / jnp.sum(codes, axis=-1, keepdims=True)
    names = expert_ids[0][:, :, None] == jnp.arange(LANES, dtype=jnp.int32)[None, None, :]
    table = jnp.sum(jnp.where(names, mixing[:, :, None], 0.0), axis=1)
    tables = lax.all_gather(table, ("expert", "tensor"), axis=0, tiled=True)
    mine = jnp.arange(LANES, dtype=jnp.int32)[None, :] == me
    weight = jnp.sum(jnp.where(mine, tables, 0.0), axis=1).reshape(EXPERTS, tokens)
    offsets = jnp.array([0, -1, 2, 1], dtype=jnp.int32)
    rows = (my_row + offsets) % SIDE
    cols = (my_col + offsets) % SIDE
    from_first = (rows[:, None] * SIDE + cols[None, :]).reshape(-1)
    from_second = (rows[None, :] * SIDE + cols[:, None]).reshape(-1)
    weight_first = jnp.take(weight[:, :half], from_first, axis=0).reshape(SIDE, SIDE * half)
    weight_second = jnp.take(weight[:, half:], from_second, axis=0).reshape(SIDE, SIDE * half)

    partial = jnp.dot(attn_heads[0], out_proj, preferred_element_type=jnp.float32)
    hidden = own_residual.astype(jnp.float32) + reduce_over_tensor(partial)
    normed = normalize(hidden, norm_gain)
    group = lax.all_to_all(
        jnp.tile(normed, (tensor_count, 1)), "tensor", split_axis=0, concat_axis=0, tiled=True
    )

    def expert(parts, weights):
        x = jnp.concatenate(parts)
        scale = jnp.concatenate(weights)[:, None]
        gate_value = jnp.einsum("rd,fd->rf", x, w_gate[0], preferred_element_type=jnp.float32)
        up_value = jnp.einsum("rd,fd->rf", x, w_up[0], preferred_element_type=jnp.float32)
        activated = (jax.nn.silu(gate_value) * up_value).astype(jnp.bfloat16)
        activated = lax.optimization_barrier(activated)
        down = jnp.dot(activated, w_down[0], preferred_element_type=jnp.float32)
        return (down * scale).astype(jnp.bfloat16)

    near, far = spread(group[:half], "x", group[half:], "y")
    first = jnp.concatenate([group[:half], near[0], far[0], far[1], near[1]])
    second = jnp.concatenate([group[half:], near[2], far[2], far[3], near[3]])
    first, second = together(first, second)
    near, far = spread(first, "y", second, "x")

    out_own = expert([first, second], [weight_first[0], weight_second[0]])
    out_near = expert(
        [near[0], near[1], near[2], near[3]],
        [weight_first[1], weight_first[3], weight_second[1], weight_second[3]],
    )
    out_far = expert(
        [far[0], far[1], far[2], far[3]],
        [weight_first[2], weight_second[2]],
    )
    size = SIDE * half
    first_sum, second_sum = collect(
        (out_own[:size], out_near[:size], out_far[:size], out_near[size : 2 * size]),
        "y",
        (out_own[size:], out_near[2 * size : 3 * size], out_far[size:], out_near[3 * size :]),
        "x",
    )
    first_sum = first_sum.astype(jnp.bfloat16).reshape(SIDE, half, model_width)
    second_sum = second_sum.astype(jnp.bfloat16).reshape(SIDE, half, model_width)
    first_mix, second_mix = collect(
        tuple(first_sum[i] for i in range(SIDE)),
        "x",
        tuple(second_sum[i] for i in range(SIDE)),
        "y",
    )
    mixed = jnp.concatenate([first_mix, second_mix])
    layer_out = (hidden + reduce_over_tensor(mixed)).astype(jnp.bfloat16)
    return layer_out[None]


def solution(mesh):
    return jax.shard_map(
        on_device,
        mesh=mesh,
        in_specs=(
            P(("dp", "expert"), None, "tensor"),
            P("tensor", None),
            P(("dp", "expert"), "tensor", None),
            P(),
            P(("dp", "expert"), "tensor", None),
            P(("dp", "expert"), "tensor", None),
            P("expert", "tensor", None),
            P("expert", "tensor", None),
            P("expert", "tensor", None),
        ),
        out_specs=P(("dp", "expert"), "tensor", None),
        check_vma=False,
    )
```

```python
import jax
import jax.numpy as jnp
from jax import lax
from jax.sharding import PartitionSpec as P

EXPERTS = 16
SIDE = 4
LANES = 128


def normalize(hidden, norm_gain):
    mean_square = jnp.mean(hidden * hidden, axis=-1, keepdims=True)
    return (hidden * lax.rsqrt(mean_square + 1e-06) * norm_gain).astype(jnp.bfloat16)


def together(*values):
    return lax.optimization_barrier(values)


def reduce_over_tensor(partial):
    count = lax.axis_size("tensor")
    parts = lax.all_to_all(
        partial.astype(jnp.bfloat16), "tensor", split_axis=0, concat_axis=0, tiled=True
    )
    parts = parts.reshape(count, partial.shape[0] // count, partial.shape[1])
    return jnp.sum(parts.astype(jnp.float32), axis=0)


def shift(value, turn, step):
    pairs = []
    for half in range(lax.axis_size("dp")):
        for row in range(SIDE):
            for col in range(SIDE):
                if (half + turn) % 2:
                    to_row, to_col = (row + step) % SIDE, col
                else:
                    to_row, to_col = row, (col + step) % SIDE
                base = half * SIDE * SIDE
                pairs.append((base + row * SIDE + col, base + to_row * SIDE + to_col))
    return lax.ppermute(value, ("dp", "expert"), pairs)


def spread(block, turn):
    half = block.shape[0] // 2
    back, front = together(shift(block, turn, 1), shift(block, turn, -1))
    far = together(shift(back[:half], turn, 1), shift(front[half:], turn, -1))
    return back, front, far[0], far[1]


def add(*values):
    total = values[0].astype(jnp.float32)
    for value in values[1:]:
        total = total + value.astype(jnp.float32)
    return total


def collect(own, back, front, far_low, far_high, turn):
    half = far_low.shape[0]
    up, down = together(shift(far_low, turn, 1), shift(far_high, turn, -1))
    front = jnp.concatenate([add(front[:half], up).astype(jnp.bfloat16), front[half:]])
    back = jnp.concatenate([back[:half], add(back[half:], down).astype(jnp.bfloat16)])
    from_back, from_front = together(shift(front, turn, 1), shift(back, turn, -1))
    return add(own, from_back, from_front)


def on_device(
    attn_heads, out_proj, residual, norm_gain, expert_ids, weight_codes, w_gate, w_up, w_down
):
    tensor_count = lax.axis_size("tensor")
    own_residual = residual[0]
    tok_own, model_width = own_residual.shape
    tokens = tok_own * tensor_count
    me = lax.axis_index("expert")

    lane = jnp.arange(LANES, dtype=jnp.int32)
    codes = weight_codes[0]
    names = expert_ids[0][:, :, None] == lane[None, None, :]
    table = jnp.sum(jnp.where(names, codes[:, :, None], 0), axis=1)
    table = table + jnp.where(lane == EXPERTS, jnp.sum(codes, axis=1, keepdims=True), 0)

    partial = jnp.dot(attn_heads[0], out_proj, preferred_element_type=jnp.float32)
    hidden = own_residual.astype(jnp.float32) + reduce_over_tensor(partial)
    normed = normalize(hidden, norm_gain)
    rows = jnp.concatenate([normed, table.astype(jnp.bfloat16)], axis=1)
    group = lax.all_to_all(
        jnp.tile(rows, (tensor_count, 1)), "tensor", split_axis=0, concat_axis=0, tiled=True
    )

    def expert(rows):
        x = rows[:, :model_width]
        tail = rows[:, model_width:].astype(jnp.float32)
        code = jnp.sum(jnp.where(lane == me, tail, 0.0), axis=1, keepdims=True)
        total = jnp.sum(jnp.where(lane == EXPERTS, tail, 0.0), axis=1, keepdims=True)
        gate_value = jnp.einsum("rd,fd->rf", x, w_gate[0], preferred_element_type=jnp.float32)
        up_value = jnp.einsum("rd,fd->rf", x, w_up[0], preferred_element_type=jnp.float32)
        activated = (jax.nn.silu(gate_value) * up_value).astype(jnp.bfloat16)
        activated = lax.optimization_barrier(activated)
        down = jnp.dot(activated, w_down[0], preferred_element_type=jnp.float32)
        return (down * (code / total)).astype(jnp.bfloat16)

    back, front, far_low, far_high = spread(group, 0)
    line = lax.optimization_barrier(jnp.concatenate([group, back, front, far_low, far_high]))
    blocks = (line, *spread(line, 1))
    line_sum = collect(*(expert(block) for block in blocks), 1).astype(jnp.bfloat16)
    edges = [0, tokens, 2 * tokens, 3 * tokens, 3 * tokens + tokens // 2, 4 * tokens]
    mixed = collect(*(line_sum[i:j] for i, j in zip(edges[:-1], edges[1:])), 0)
    layer_out = (hidden + reduce_over_tensor(mixed)).astype(jnp.bfloat16)
    return layer_out[None]


def solution(mesh):
    return jax.shard_map(
        on_device,
        mesh=mesh,
        in_specs=(
            P(("dp", "expert"), None, "tensor"),
            P("tensor", None),
            P(("dp", "expert"), "tensor", None),
            P(),
            P(("dp", "expert"), "tensor", None),
            P(("dp", "expert"), "tensor", None),
            P("expert", "tensor", None),
            P("expert", "tensor", None),
            P("expert", "tensor", None),
        ),
        out_specs=P(("dp", "expert"), "tensor", None),
        check_vma=False,
    )
```

```python
import jax
import jax.numpy as jnp
from jax import lax
from jax.sharding import PartitionSpec as P

EXPERTS = 16
SIDE = 4
LANES = 128


def normalize(hidden, norm_gain):
    mean_square = jnp.mean(hidden * hidden, axis=-1, keepdims=True)
    return (hidden * lax.rsqrt(mean_square + 1e-06) * norm_gain).astype(jnp.bfloat16)


def reduce_over_tensor(partial):
    count = lax.axis_size("tensor")
    parts = lax.all_to_all(
        partial.astype(jnp.bfloat16), "tensor", split_axis=0, concat_axis=0, tiled=True
    )
    parts = parts.reshape(count, partial.shape[0] // count, partial.shape[1])
    return jnp.sum(parts.astype(jnp.float32), axis=0)


def shift(value, turn, step):
    pairs = []
    for half in range(lax.axis_size("dp")):
        for row in range(SIDE):
            for col in range(SIDE):
                if (half + turn) % 2:
                    to_row, to_col = (row + step) % SIDE, col
                else:
                    to_row, to_col = row, (col + step) % SIDE
                base = half * SIDE * SIDE
                pairs.append((base + row * SIDE + col, base + to_row * SIDE + to_col))
    return lax.ppermute(value, ("dp", "expert"), pairs)


def send_round(block, turn):
    return shift(block, turn, 1), shift(block, turn, -1)


def send_on(back, front, turn):
    half = back.shape[0] // 2
    return shift(back[:half], turn, 1), shift(front[half:], turn, -1)


def add(*values):
    total = values[0].astype(jnp.float32)
    for value in values[1:]:
        total = total + value.astype(jnp.float32)
    return total


def collect(own, back, front, far_low, far_high, turn):
    half = far_low.shape[0]
    up, down = shift(far_low, turn, 1), shift(far_high, turn, -1)
    front = jnp.concatenate([add(front[:half], up).astype(jnp.bfloat16), front[half:]])
    back = jnp.concatenate([back[:half], add(back[half:], down).astype(jnp.bfloat16)])
    return add(own, shift(front, turn, 1), shift(back, turn, -1))


def on_device(
    attn_heads, out_proj, residual, norm_gain, expert_ids, weight_codes, w_gate, w_up, w_down
):
    tensor_count = lax.axis_size("tensor")
    own_residual = residual[0]
    tok_own, model_width = own_residual.shape
    tokens = tok_own * tensor_count
    me = lax.axis_index("expert")

    lane = jnp.arange(LANES, dtype=jnp.int32)
    codes = weight_codes[0]
    names = expert_ids[0][:, :, None] == lane[None, None, :]
    table = jnp.sum(jnp.where(names, codes[:, :, None], 0), axis=1)
    table = table + jnp.where(lane == EXPERTS, jnp.sum(codes, axis=1, keepdims=True), 0)

    partial = jnp.dot(attn_heads[0], out_proj, preferred_element_type=jnp.float32)
    hidden = own_residual.astype(jnp.float32) + reduce_over_tensor(partial)
    normed = normalize(hidden, norm_gain)
    rows = jnp.concatenate([normed, table.astype(jnp.bfloat16)], axis=1)
    group = lax.all_to_all(
        jnp.tile(rows, (tensor_count, 1)), "tensor", split_axis=0, concat_axis=0, tiled=True
    )

    def expert(rows, who):
        x = rows[:, :model_width]
        tail = rows[:, model_width:].astype(jnp.float32)
        code = jnp.sum(jnp.where(lane == who, tail, 0.0), axis=1, keepdims=True)
        total = jnp.sum(jnp.where(lane == EXPERTS, tail, 0.0), axis=1, keepdims=True)
        gate_value = jnp.einsum("rd,fd->rf", x, w_gate[0], preferred_element_type=jnp.float32)
        up_value = jnp.einsum("rd,fd->rf", x, w_up[0], preferred_element_type=jnp.float32)
        activated = (jax.nn.silu(gate_value) * up_value).astype(jnp.bfloat16)
        activated = lax.optimization_barrier(activated)
        scale = code / total
        down = jnp.dot(activated, w_down[0], preferred_element_type=jnp.float32)
        return (down * scale).astype(jnp.bfloat16), scale

    def pieces(block):
        back, front = send_round(block, 1)
        return (block, back, front, *send_on(back, front, 1))

    back, front = send_round(group, 0)
    far = send_on(back, front, 0)
    first = pieces(jnp.concatenate([group, back]))
    second = pieces(jnp.concatenate([front, *far]))
    first_out = [expert(block, me) for block in first]
    late = me + (first_out[4][1][0, 0] < 0.0).astype(jnp.int32)
    second_out = [expert(block, who) for block, who in zip(second, (me, me, me, late, late))]
    first_sum = collect(*(out for out, _ in first_out), 1).astype(jnp.bfloat16)
    second_sum = collect(*(out for out, _ in second_out), 1).astype(jnp.bfloat16)
    half = tokens // 2
    mixed = collect(
        first_sum[:tokens],
        first_sum[tokens:],
        second_sum[:tokens],
        second_sum[tokens : tokens + half],
        second_sum[tokens + half :],
        0,
    )
    layer_out = (hidden + reduce_over_tensor(mixed)).astype(jnp.bfloat16)
    return layer_out[None]


def solution(mesh):
    return jax.shard_map(
        on_device,
        mesh=mesh,
        in_specs=(
            P(("dp", "expert"), None, "tensor"),
            P("tensor", None),
            P(("dp", "expert"), "tensor", None),
            P(),
            P(("dp", "expert"), "tensor", None),
            P(("dp", "expert"), "tensor", None),
            P("expert", "tensor", None),
            P("expert", "tensor", None),
            P("expert", "tensor", None),
        ),
        out_specs=P(("dp", "expert"), "tensor", None),
        check_vma=False,
    )
```

```python
import functools

import jax
import jax.numpy as jnp
from jax import lax
from jax.experimental import pallas as pl
from jax.experimental.pallas import tpu as pltpu
from jax.sharding import PartitionSpec as P

EXPERTS = 16
SIDE = 4
LANES = 128
CHUNK = 1024


def normalize(hidden, norm_gain):
    mean_square = jnp.mean(hidden * hidden, axis=-1, keepdims=True)
    return (hidden * lax.rsqrt(mean_square + 1e-06) * norm_gain).astype(jnp.bfloat16)


def reduce_over_tensor(partial):
    count = lax.axis_size("tensor")
    parts = lax.all_to_all(
        partial.astype(jnp.bfloat16), "tensor", split_axis=0, concat_axis=0, tiled=True
    )
    parts = parts.reshape(count, partial.shape[0] // count, partial.shape[1])
    return jnp.sum(parts.astype(jnp.float32), axis=0)


def shift(value, turn, step):
    pairs = []
    for half in range(lax.axis_size("dp")):
        for row in range(SIDE):
            for col in range(SIDE):
                if (half + turn) % 2:
                    to_row, to_col = (row + step) % SIDE, col
                else:
                    to_row, to_col = row, (col + step) % SIDE
                base = half * SIDE * SIDE
                pairs.append((base + row * SIDE + col, base + to_row * SIDE + to_col))
    return lax.ppermute(value, ("dp", "expert"), pairs)


def send_round(block, turn):
    return shift(block, turn, 1), shift(block, turn, -1)


def send_on(back, front, turn):
    half = back.shape[0] // 2
    return shift(back[:half], turn, 1), shift(front[half:], turn, -1)


def add(*values):
    total = values[0].astype(jnp.float32)
    for value in values[1:]:
        total = total + value.astype(jnp.float32)
    return total


def collect(own, back, front, far_low, far_high, turn):
    half = far_low.shape[0]
    up, down = shift(far_low, turn, 1), shift(far_high, turn, -1)
    front = jnp.concatenate([add(front[:half], up).astype(jnp.bfloat16), front[half:]])
    back = jnp.concatenate([back[:half], add(back[half:], down).astype(jnp.bfloat16)])
    return add(own, shift(front, turn, 1), shift(back, turn, -1))


def expert_kernel(count, me_ref, *refs):
    blocks, (gate_ref, up_ref, down_ref), outs = refs[:count], refs[count : count + 3], refs[count + 3 :]
    width = gate_ref.shape[1]
    x = jnp.concatenate([block[:, :width] for block in blocks])
    tail = jnp.concatenate([block[:, width:] for block in blocks]).astype(jnp.float32)
    lane = lax.broadcasted_iota(jnp.int32, tail.shape, 1)
    code = jnp.sum(jnp.where(lane == me_ref[0], tail, 0.0), axis=1, keepdims=True)
    total = jnp.sum(jnp.where(lane == EXPERTS, tail, 0.0), axis=1, keepdims=True)
    both_last = (((1,), (1,)), ((), ()))
    gate_value = lax.dot_general(x, gate_ref[...], both_last, preferred_element_type=jnp.float32)
    up_value = lax.dot_general(x, up_ref[...], both_last, preferred_element_type=jnp.float32)
    activated = (jax.nn.silu(gate_value) * up_value).astype(jnp.bfloat16)
    scale = code / total
    size = outs[0].shape[0]
    for start in range(0, width, CHUNK):
        down = jnp.dot(
            activated, down_ref[:, start : start + CHUNK], preferred_element_type=jnp.float32
        )
        result = (down * scale).astype(jnp.bfloat16)
        for i, out in enumerate(outs):
            out[:, start : start + CHUNK] = result[i * size : (i + 1) * size]


def run_expert(me, blocks, w_gate, w_up, w_down):
    count, size = len(blocks), blocks[0].shape[0]
    units, width = w_gate.shape
    vmem = pl.BlockSpec(memory_space=pltpu.VMEM)
    return pl.pallas_call(
        functools.partial(expert_kernel, count),
        out_shape=[jax.ShapeDtypeStruct((size, width), jnp.bfloat16)] * count,
        in_specs=[pl.BlockSpec(memory_space=pltpu.SMEM)] + [vmem] * (count + 3),
        out_specs=[vmem] * count,
        compiler_params=pltpu.CompilerParams(vmem_limit_bytes=20 << 20),
        cost_estimate=pl.CostEstimate(
            flops=6 * count * size * units * width,
            bytes_accessed=4 * count * size * width + 6 * units * width,
            transcendentals=count * size * units,
        ),
    )(me, *blocks, w_gate, w_up, w_down)


def on_device(
    attn_heads, out_proj, residual, norm_gain, expert_ids, weight_codes, w_gate, w_up, w_down
):
    tensor_count = lax.axis_size("tensor")
    own_residual = residual[0]
    tok_own, model_width = own_residual.shape
    tokens = tok_own * tensor_count
    me = lax.axis_index("expert")

    lane = jnp.arange(LANES, dtype=jnp.int32)
    codes = weight_codes[0]
    names = expert_ids[0][:, :, None] == lane[None, None, :]
    table = jnp.sum(jnp.where(names, codes[:, :, None], 0), axis=1)
    table = table + jnp.where(lane == EXPERTS, jnp.sum(codes, axis=1, keepdims=True), 0)

    partial = jnp.dot(attn_heads[0], out_proj, preferred_element_type=jnp.float32)
    hidden = own_residual.astype(jnp.float32) + reduce_over_tensor(partial)
    normed = normalize(hidden, norm_gain)
    rows = jnp.concatenate([normed, table.astype(jnp.bfloat16)], axis=1)
    group = lax.all_to_all(
        jnp.tile(rows, (tensor_count, 1)), "tensor", split_axis=0, concat_axis=0, tiled=True
    )

    weights = (w_gate[0], w_up[0], w_down[0])
    who = jnp.reshape(me, (1,)).astype(jnp.int32)

    def experts(*blocks):
        return run_expert(who, blocks, *weights)

    def tie(values, others):
        tied = lax.optimization_barrier((*values, *others))
        return tied[: len(values)], tied[len(values) :]

    back, front = send_round(group, 0)
    first = jnp.concatenate([group, back])
    first_near = send_round(first, 1)
    far = send_on(back, front, 0)
    first_own = experts(first)
    second = jnp.concatenate([front, *far])
    (second,), first_own = tie((second,), first_own)
    second_near = send_round(second, 1)
    second_own = experts(second)
    first_near, second_own = tie(first_near, second_own)
    first_far = send_on(*first_near, 1)
    first_near_out = experts(*first_near)
    second_near, first_near_out = tie(second_near, first_near_out)
    second_far = send_on(*second_near, 1)
    first_far_out = experts(*first_far)
    second_near, first_far_out = tie(second_near, first_far_out)
    second_near_out = experts(*second_near)
    second_far, second_near_out = tie(second_far, second_near_out)
    second_far_out = experts(*second_far)
    first_sum = collect(*first_own, *first_near_out, *first_far_out, 1).astype(jnp.bfloat16)
    second_sum = collect(*second_own, *second_near_out, *second_far_out, 1).astype(jnp.bfloat16)
    half = tokens // 2
    mixed = collect(
        first_sum[:tokens],
        first_sum[tokens:],
        second_sum[:tokens],
        second_sum[tokens : tokens + half],
        second_sum[tokens + half :],
        0,
    )
    layer_out = (hidden + reduce_over_tensor(mixed)).astype(jnp.bfloat16)
    return layer_out[None]


def solution(mesh):
    return jax.shard_map(
        on_device,
        mesh=mesh,
        in_specs=(
            P(("dp", "expert"), None, "tensor"),
            P("tensor", None),
            P(("dp", "expert"), "tensor", None),
            P(),
            P(("dp", "expert"), "tensor", None),
            P(("dp", "expert"), "tensor", None),
            P("expert", "tensor", None),
            P("expert", "tensor", None),
            P("expert", "tensor", None),
        ),
        out_specs=P(("dp", "expert"), "tensor", None),
        check_vma=False,
    )
```

```python
import functools

import jax
import jax.numpy as jnp
from jax import lax
from jax.experimental import pallas as pl
from jax.experimental.pallas import tpu as pltpu
from jax.sharding import PartitionSpec as P

EXPERTS = 16
SIDE = 4
LANES = 128
CHUNK = 1024
GRANT = 8 << 20


def vmem_spec():
    return pl.BlockSpec(memory_space=pltpu.VMEM)


def project_kernel(heads_ref, proj_ref, out_ref):
    out_ref[...] = jnp.dot(
        heads_ref[...], proj_ref[...], preferred_element_type=jnp.float32
    ).astype(jnp.bfloat16)


def project(heads, proj):
    tokens, features = heads.shape
    width = proj.shape[1]
    return pl.pallas_call(
        project_kernel,
        grid=(width // CHUNK,),
        out_shape=jax.ShapeDtypeStruct((tokens, width), jnp.bfloat16),
        in_specs=[
            pl.BlockSpec((tokens, features), lambda i: (0, 0)),
            pl.BlockSpec((features, CHUNK), lambda i: (0, i)),
        ],
        out_specs=pl.BlockSpec((tokens, CHUNK), lambda i: (0, i)),
        compiler_params=pltpu.CompilerParams(vmem_limit_bytes=GRANT),
        cost_estimate=pl.CostEstimate(
            flops=2 * tokens * features * width,
            bytes_accessed=2 * features * width,
            transcendentals=0,
        ),
    )(heads, proj)


def norm_kernel(count, parts_ref, residual_ref, gain_ref, ids_ref, codes_ref, hidden_ref, rows_ref):
    size, width = residual_ref.shape
    hidden = residual_ref[...].astype(jnp.float32)
    attn = parts_ref[:size].astype(jnp.float32)
    for i in range(1, count):
        attn = attn + parts_ref[i * size : (i + 1) * size].astype(jnp.float32)
    hidden = hidden + attn
    hidden_ref[...] = hidden
    mean_square = jnp.mean(hidden * hidden, axis=-1, keepdims=True)
    normed = (hidden * lax.rsqrt(mean_square + 1e-06) * gain_ref[...]).astype(jnp.bfloat16)
    ids, codes = ids_ref[...], codes_ref[...]
    lane = lax.broadcasted_iota(jnp.int32, (size, LANES), 1)
    table = jnp.zeros((size, LANES), jnp.int32)
    for k in range(ids.shape[1]):
        code = codes[:, k : k + 1]
        table = table + jnp.where((lane == ids[:, k : k + 1]) | (lane == EXPERTS), code, 0)
    table = table.astype(jnp.float32).astype(jnp.bfloat16)
    for i in range(count):
        rows_ref[i * size : (i + 1) * size, :width] = normed
        rows_ref[i * size : (i + 1) * size, width:] = table


def normalize(parts, residual, gain, ids, codes, count):
    size, width = residual.shape
    return pl.pallas_call(
        functools.partial(norm_kernel, count),
        out_shape=[
            jax.ShapeDtypeStruct((size, width), jnp.float32),
            jax.ShapeDtypeStruct((count * size, width + LANES), jnp.bfloat16),
        ],
        in_specs=[vmem_spec()] * 5,
        out_specs=[vmem_spec()] * 2,
        compiler_params=pltpu.CompilerParams(vmem_limit_bytes=GRANT),
        cost_estimate=pl.CostEstimate(
            flops=20 * size * width, bytes_accessed=6 * count * size * width, transcendentals=size
        ),
    )(parts, residual, gain, ids, codes)


def swap_over_tensor(value):
    return lax.all_to_all(value, "tensor", split_axis=0, concat_axis=0, tiled=True)


def shift(value, turn, step):
    pairs = []
    for half in range(lax.axis_size("dp")):
        for row in range(SIDE):
            for col in range(SIDE):
                if (half + turn) % 2:
                    to_row, to_col = (row + step) % SIDE, col
                else:
                    to_row, to_col = row, (col + step) % SIDE
                base = half * SIDE * SIDE
                pairs.append((base + row * SIDE + col, base + to_row * SIDE + to_col))
    return lax.ppermute(value, ("dp", "expert"), pairs)


def send_round(block, turn):
    return shift(block, turn, 1), shift(block, turn, -1)


def send_on(back, front, turn):
    half = back.shape[0] // 2
    return shift(back[:half], turn, 1), shift(front[half:], turn, -1)


def add(*values):
    total = values[0].astype(jnp.float32)
    for value in values[1:]:
        total = total + value.astype(jnp.float32)
    return total


def tie(values, others):
    tied = lax.optimization_barrier((*values, *others))
    return tied[: len(values)], tied[len(values) :]


def plus(*values):
    return add(*values).astype(jnp.bfloat16)


def expert_kernel(count, me_ref, *refs):
    blocks, (gate_ref, up_ref, down_ref), outs = refs[:count], refs[count : count + 3], refs[count + 3 :]
    width = gate_ref.shape[1]
    x = jnp.concatenate([block[:, :width] for block in blocks])
    tail = jnp.concatenate([block[:, width:] for block in blocks]).astype(jnp.float32)
    lane = lax.broadcasted_iota(jnp.int32, tail.shape, 1)
    code = jnp.sum(jnp.where(lane == me_ref[0], tail, 0.0), axis=1, keepdims=True)
    total = jnp.sum(jnp.where(lane == EXPERTS, tail, 0.0), axis=1, keepdims=True)
    both_last = (((1,), (1,)), ((), ()))
    gate_value = lax.dot_general(x, gate_ref[...], both_last, preferred_element_type=jnp.float32)
    up_value = lax.dot_general(x, up_ref[...], both_last, preferred_element_type=jnp.float32)
    activated = (jax.nn.silu(gate_value) * up_value).astype(jnp.bfloat16)
    scale = code / total
    size = outs[0].shape[0]
    for start in range(0, width, CHUNK):
        down = jnp.dot(
            activated, down_ref[:, start : start + CHUNK], preferred_element_type=jnp.float32
        )
        result = (down * scale).astype(jnp.bfloat16)
        for i, out in enumerate(outs):
            out[:, start : start + CHUNK] = result[i * size : (i + 1) * size]


def run_expert(me, blocks, size, w_gate, w_up, w_down):
    count = len(blocks)
    pieces = count * blocks[0].shape[0] // size
    units, width = w_gate.shape
    vmem = pl.BlockSpec(memory_space=pltpu.VMEM)
    return pl.pallas_call(
        functools.partial(expert_kernel, count),
        out_shape=[jax.ShapeDtypeStruct((size, width), jnp.bfloat16)] * pieces,
        in_specs=[pl.BlockSpec(memory_space=pltpu.SMEM)] + [vmem] * (count + 3),
        out_specs=[vmem] * pieces,
        compiler_params=pltpu.CompilerParams(vmem_limit_bytes=GRANT),
        cost_estimate=pl.CostEstimate(
            flops=6 * pieces * size * units * width,
            bytes_accessed=4 * pieces * size * width + 6 * units * width,
            transcendentals=pieces * size * units,
        ),
    )(me, *blocks, w_gate, w_up, w_down)


def on_device(
    attn_heads, out_proj, residual, norm_gain, expert_ids, weight_codes, w_gate, w_up, w_down
):
    tensor_count = lax.axis_size("tensor")
    me = lax.axis_index("expert")
    partial = project(attn_heads[0], out_proj)
    hidden, rows = normalize(
        swap_over_tensor(partial),
        residual[0],
        norm_gain[None],
        expert_ids[0],
        weight_codes[0],
        tensor_count,
    )
    group = swap_over_tensor(rows)
    tokens, model_width = partial.shape

    weights = (w_gate[0], w_up[0], w_down[0])
    who = jnp.reshape(me, (1,)).astype(jnp.int32)

    def experts(*blocks):
        return run_expert(who, blocks, tokens, *weights)

    def both(ahead, behind, turn):
        return [shift(ahead, turn, 1), shift(behind, turn, -1)]

    back, front = send_round(group, 0)
    first = jnp.concatenate([group, back])
    first_near = send_round(first, 1)
    far = send_on(back, front, 0)
    first_own = experts(first)
    second = jnp.concatenate([front, *far])
    (second,), first_own = tie((second,), first_own)
    second_near = send_round(second, 1)
    second_own = experts(second)
    first_near, second_own = tie(first_near, second_own)
    first_far = send_on(*first_near, 1)
    a_back_low, a_back_high, a_front_low, a_front_high = experts(*first_near)
    second_near, (a_back_low, a_front_high) = tie(second_near, (a_back_low, a_front_high))
    second_far = send_on(*second_near, 1)
    a_far = experts(*first_far)
    second_near, a_far = tie(second_near, a_far)
    a_up, a_down = both(*a_far, 1)
    b_back_low, b_back_high, b_front_low, b_front_high = experts(*second_near)
    second_far, (b_back_low, b_front_high) = tie(second_far, (b_back_low, b_front_high))
    b_far = experts(*second_far)
    b_up, b_down = both(*b_far, 1)

    a_got = both(a_front_high, a_back_low, 1)
    b_got = both(b_front_high, b_back_low, 1)
    a_late = both(plus(a_front_low, a_up), plus(a_back_high, a_down), 1)
    b_late = both(plus(b_front_low, b_up), plus(b_back_high, b_down), 1)
    far = plus(second_own[1], b_got[0], b_late[1])
    front = plus(second_own[0], b_late[0], b_got[1])
    back = plus(first_own[1], a_got[0], a_late[1])
    own = plus(first_own[0], a_late[0], a_got[1])

    half = tokens // 2
    up, down = both(far[:half], far[half:], 0)
    got = both(front[half:], back[:half], 0)
    late = both(plus(front[:half], up), plus(back[half:], down), 0)
    mixed = jnp.concatenate([plus(own[:half], late[0], got[1]), plus(own[half:], got[0], late[1])])
    parts = swap_over_tensor(mixed).reshape(tensor_count, -1, model_width)
    layer_out = (hidden + jnp.sum(parts.astype(jnp.float32), axis=0)).astype(jnp.bfloat16)
    return layer_out[None]


def solution(mesh):
    return jax.shard_map(
        on_device,
        mesh=mesh,
        in_specs=(
            P(("dp", "expert"), None, "tensor"),
            P("tensor", None),
            P(("dp", "expert"), "tensor", None),
            P(),
            P(("dp", "expert"), "tensor", None),
            P(("dp", "expert"), "tensor", None),
            P("expert", "tensor", None),
            P("expert", "tensor", None),
            P("expert", "tensor", None),
        ),
        out_specs=P(("dp", "expert"), "tensor", None),
        check_vma=False,
    )
```

```python
import functools

import jax
import jax.numpy as jnp
from jax import lax
from jax.experimental import pallas as pl
from jax.experimental.pallas import tpu as pltpu
from jax.sharding import PartitionSpec as P

EXPERTS = 16
SIDE = 4
LANES = 128
CHUNK = 1024
GRANT = 8 << 20
STREAM = 62 << 20


def vmem_spec():
    return pl.BlockSpec(memory_space=pltpu.VMEM)


def project_kernel(heads_ref, proj_ref, out_ref):
    out_ref[...] = jnp.dot(
        heads_ref[...], proj_ref[...], preferred_element_type=jnp.float32
    ).astype(jnp.bfloat16)


def project(heads, proj):
    tokens, features = heads.shape
    width = proj.shape[1]
    return pl.pallas_call(
        project_kernel,
        grid=(width // CHUNK,),
        out_shape=jax.ShapeDtypeStruct((tokens, width), jnp.bfloat16),
        in_specs=[
            pl.BlockSpec((tokens, features), lambda i: (0, 0)),
            pl.BlockSpec((features, CHUNK), lambda i: (0, i)),
        ],
        out_specs=pl.BlockSpec((tokens, CHUNK), lambda i: (0, i)),
        compiler_params=pltpu.CompilerParams(vmem_limit_bytes=STREAM),
        cost_estimate=pl.CostEstimate(
            flops=2 * tokens * features * width,
            bytes_accessed=2 * features * width,
            transcendentals=0,
        ),
    )(heads, proj)


def norm_kernel(count, parts_ref, residual_ref, gain_ref, ids_ref, codes_ref, hidden_ref, rows_ref):
    size, width = residual_ref.shape
    hidden = residual_ref[...].astype(jnp.float32)
    attn = parts_ref[:size].astype(jnp.float32)
    for i in range(1, count):
        attn = attn + parts_ref[i * size : (i + 1) * size].astype(jnp.float32)
    hidden = hidden + attn
    hidden_ref[...] = hidden
    mean_square = jnp.mean(hidden * hidden, axis=-1, keepdims=True)
    normed = (hidden * lax.rsqrt(mean_square + 1e-06) * gain_ref[...]).astype(jnp.bfloat16)
    ids, codes = ids_ref[...], codes_ref[...]
    lane = lax.broadcasted_iota(jnp.int32, (size, LANES), 1)
    table = jnp.zeros((size, LANES), jnp.int32)
    for k in range(ids.shape[1]):
        code = codes[:, k : k + 1]
        table = table + jnp.where((lane == ids[:, k : k + 1]) | (lane == EXPERTS), code, 0)
    table = table.astype(jnp.float32).astype(jnp.bfloat16)
    for i in range(count):
        rows_ref[i * size : (i + 1) * size, :width] = normed
        rows_ref[i * size : (i + 1) * size, width:] = table


def normalize(parts, residual, gain, ids, codes, count):
    size, width = residual.shape
    return pl.pallas_call(
        functools.partial(norm_kernel, count),
        out_shape=[
            jax.ShapeDtypeStruct((size, width), jnp.float32),
            jax.ShapeDtypeStruct((count * size, width + LANES), jnp.bfloat16),
        ],
        in_specs=[vmem_spec()] * 5,
        out_specs=[vmem_spec()] * 2,
        compiler_params=pltpu.CompilerParams(vmem_limit_bytes=GRANT),
        cost_estimate=pl.CostEstimate(
            flops=20 * size * width, bytes_accessed=6 * count * size * width, transcendentals=size
        ),
    )(parts, residual, gain, ids, codes)


def swap_over_tensor(value):
    return lax.all_to_all(value, "tensor", split_axis=0, concat_axis=0, tiled=True)


def shift(value, turn, step):
    pairs = []
    for half in range(lax.axis_size("dp")):
        for row in range(SIDE):
            for col in range(SIDE):
                if (half + turn) % 2:
                    to_row, to_col = (row + step) % SIDE, col
                else:
                    to_row, to_col = row, (col + step) % SIDE
                base = half * SIDE * SIDE
                pairs.append((base + row * SIDE + col, base + to_row * SIDE + to_col))
    return lax.ppermute(value, ("dp", "expert"), pairs)


def send_round(block, turn):
    return shift(block, turn, 1), shift(block, turn, -1)


def send_on(back, front, turn):
    half = back.shape[0] // 2
    return shift(back[:half], turn, 1), shift(front[half:], turn, -1)


def add(*values):
    total = values[0].astype(jnp.float32)
    for value in values[1:]:
        total = total + value.astype(jnp.float32)
    return total


def tie(values, others):
    tied = lax.optimization_barrier((*values, *others))
    return tied[: len(values)], tied[len(values) :]


def join(back, front, up, down):
    half = up.shape[0]
    front = jnp.concatenate([add(front[:half], up).astype(jnp.bfloat16), front[half:]])
    back = jnp.concatenate([back[:half], add(back[half:], down).astype(jnp.bfloat16)])
    return front, back


def pair_kernel(own_ref, back_ref, front_ref, pair_ref, low_ref, high_ref):
    size, half = own_ref.shape[0], low_ref.shape[0]
    pair_ref[:size] = own_ref[...]
    pair_ref[size:] = back_ref[...]
    low_ref[...] = back_ref[:half]
    high_ref[...] = front_ref[half:]


def pair(own, back, front):
    size, width = own.shape
    shapes = [(2 * size, width), (size // 2, width), (size // 2, width)]
    return pl.pallas_call(
        pair_kernel,
        out_shape=[jax.ShapeDtypeStruct(shape, own.dtype) for shape in shapes],
        in_specs=[vmem_spec()] * 3,
        out_specs=[vmem_spec()] * 3,
        compiler_params=pltpu.CompilerParams(vmem_limit_bytes=GRANT),
        cost_estimate=pl.CostEstimate(flops=0, bytes_accessed=12 * size * width, transcendentals=0),
    )(own, back, front)


def expert_kernel(count, me_ref, *refs):
    blocks, (gate_ref, up_ref, down_ref), outs = refs[:count], refs[count : count + 3], refs[count + 3 :]
    width = gate_ref.shape[1]
    x = jnp.concatenate([block[:, :width] for block in blocks])
    tail = jnp.concatenate([block[:, width:] for block in blocks]).astype(jnp.float32)
    lane = lax.broadcasted_iota(jnp.int32, tail.shape, 1)
    code = jnp.sum(jnp.where(lane == me_ref[0], tail, 0.0), axis=1, keepdims=True)
    total = jnp.sum(jnp.where(lane == EXPERTS, tail, 0.0), axis=1, keepdims=True)
    both_last = (((1,), (1,)), ((), ()))
    gate_value = lax.dot_general(x, gate_ref[...], both_last, preferred_element_type=jnp.float32)
    up_value = lax.dot_general(x, up_ref[...], both_last, preferred_element_type=jnp.float32)
    activated = (jax.nn.silu(gate_value) * up_value).astype(jnp.bfloat16)
    scale = code / total
    size = outs[0].shape[0]
    for start in range(0, width, CHUNK):
        down = jnp.dot(
            activated, down_ref[:, start : start + CHUNK], preferred_element_type=jnp.float32
        )
        result = (down * scale).astype(jnp.bfloat16)
        for i, out in enumerate(outs):
            out[:, start : start + CHUNK] = result[i * size : (i + 1) * size]


def run_expert(me, blocks, w_gate, w_up, w_down):
    count, size = len(blocks), blocks[0].shape[0]
    units, width = w_gate.shape
    vmem = pl.BlockSpec(memory_space=pltpu.VMEM)
    return pl.pallas_call(
        functools.partial(expert_kernel, count),
        out_shape=[jax.ShapeDtypeStruct((size, width), jnp.bfloat16)] * count,
        in_specs=[pl.BlockSpec(memory_space=pltpu.SMEM)] + [vmem] * (count + 3),
        out_specs=[vmem] * count,
        compiler_params=pltpu.CompilerParams(vmem_limit_bytes=GRANT),
        cost_estimate=pl.CostEstimate(
            flops=6 * count * size * units * width,
            bytes_accessed=4 * count * size * width + 6 * units * width,
            transcendentals=count * size * units,
        ),
    )(me, *blocks, w_gate, w_up, w_down)


def on_device(
    attn_heads, out_proj, residual, norm_gain, expert_ids, weight_codes, w_gate, w_up, w_down
):
    tensor_count = lax.axis_size("tensor")
    who = jnp.reshape(lax.axis_index("expert"), (1,)).astype(jnp.int32)
    (heads,), (who,) = tie((attn_heads[0],), (who,))
    partial = project(heads, out_proj)
    hidden, rows = normalize(
        swap_over_tensor(partial),
        residual[0],
        norm_gain[None],
        expert_ids[0],
        weight_codes[0],
        tensor_count,
    )
    group = swap_over_tensor(rows)
    tokens, model_width = partial.shape

    weights = (w_gate[0], w_up[0], w_down[0])

    def experts(*blocks):
        return run_expert(who, blocks, *weights)

    def both(ahead, behind, turn):
        return shift(ahead, turn, 1), shift(behind, turn, -1)

    back, front = send_round(group, 0)
    first, low, high = pair(group, back, front)
    first_near = send_round(first, 1)
    far = both(low, high, 0)
    first_own = experts(first)
    second = jnp.concatenate([front, *far])
    (second,), first_own = tie((second,), first_own)
    second_near = send_round(second, 1)
    second_own = experts(second)
    first_near, second_own = tie(first_near, second_own)
    first_far = send_on(*first_near, 1)
    first_near_out = experts(*first_near)
    second_near, first_near_out = tie(second_near, first_near_out)
    second_far = send_on(*second_near, 1)
    first_far_out = experts(*first_far)
    second_far, first_far_out = tie(second_far, first_far_out)
    second_far_out = experts(*second_far)
    first_up = both(*first_far_out, 1)
    second_up = both(*second_far_out, 1)
    first_up, first_own = tie(first_up, first_own)
    first_send = join(*first_near_out, *first_up)
    second_near, first_send = tie(second_near, first_send)
    second_near_out = experts(*second_near)
    second_send = join(*second_near_out, *second_up)
    first_got = both(*first_send, 1)
    second_got = both(*second_send, 1)
    first_sum = add(*first_own, *first_got).astype(jnp.bfloat16)
    (first_sum,), second_own = tie((first_sum,), second_own)
    second_sum = add(*second_own, *second_got).astype(jnp.bfloat16)

    half = tokens // 2
    far_low, far_high = second_sum[tokens : tokens + half], second_sum[tokens + half :]
    up = both(far_low, far_high, 0)
    front, back = join(first_sum[tokens:], second_sum[:tokens], *up)
    got = both(front, back, 0)
    mixed = add(first_sum[:tokens], *got).astype(jnp.bfloat16)
    parts = swap_over_tensor(mixed).reshape(tensor_count, -1, model_width)
    layer_out = (hidden + jnp.sum(parts.astype(jnp.float32), axis=0)).astype(jnp.bfloat16)
    return layer_out[None]


def solution(mesh):
    return jax.shard_map(
        on_device,
        mesh=mesh,
        in_specs=(
            P(("dp", "expert"), None, "tensor"),
            P("tensor", None),
            P(("dp", "expert"), "tensor", None),
            P(),
            P(("dp", "expert"), "tensor", None),
            P(("dp", "expert"), "tensor", None),
            P("expert", "tensor", None),
            P("expert", "tensor", None),
            P("expert", "tensor", None),
        ),
        out_specs=P(("dp", "expert"), "tensor", None),
        check_vma=False,
    )
```

```python
import functools

import jax
import jax.numpy as jnp
from jax import lax
from jax.experimental import pallas as pl
from jax.experimental.pallas import tpu as pltpu
from jax.sharding import PartitionSpec as P

EXPERTS = 16
TOP_TOKENS, CAP = 8, 6
SIDE = 4
LANES = 128
CHUNK = 1024
STRIPE = 512
GRANT = 8 << 20
STREAM = 62 << 20


def vmem_spec():
    return pl.BlockSpec(memory_space=pltpu.VMEM)


def project_kernel(heads_hbm, proj_hbm, out_ref, heads_ref, proj_ref, sems):
    count, _, size = proj_ref.shape
    copies = [pltpu.make_async_copy(heads_hbm, heads_ref, sems.at[count])]
    for i in range(count):
        columns = pl.ds(i * size, size)
        copies.append(
            pltpu.make_async_copy(proj_hbm.at[:, columns], proj_ref.at[i], sems.at[i])
        )
    for copy in copies:
        copy.start()
    copies[0].wait()
    heads = heads_ref[...]
    for i in range(count):
        copies[i + 1].wait()
        out_ref[:, i * size : (i + 1) * size] = jnp.dot(
            heads, proj_ref[i], preferred_element_type=jnp.float32
        ).astype(jnp.bfloat16)


def project(heads, proj):
    tokens, features = heads.shape
    width = proj.shape[1]
    count = width // STRIPE
    return pl.pallas_call(
        project_kernel,
        out_shape=jax.ShapeDtypeStruct((tokens, width), jnp.bfloat16),
        in_specs=[pl.BlockSpec(memory_space=pl.ANY)] * 2,
        out_specs=vmem_spec(),
        scratch_shapes=[
            pltpu.VMEM((tokens, features), jnp.bfloat16),
            pltpu.VMEM((count, features, STRIPE), jnp.bfloat16),
            pltpu.SemaphoreType.DMA((count + 1,)),
        ],
        compiler_params=pltpu.CompilerParams(vmem_limit_bytes=STREAM),
        cost_estimate=pl.CostEstimate(
            flops=2 * tokens * features * width,
            bytes_accessed=2 * features * width,
            transcendentals=0,
        ),
    )(heads, proj)


def norm_kernel(count, parts_ref, residual_ref, gain_ref, ids_ref, codes_ref, hidden_ref, rows_ref):
    size, width = residual_ref.shape
    hidden = residual_ref[...].astype(jnp.float32)
    attn = parts_ref[:size].astype(jnp.float32)
    for i in range(1, count):
        attn = attn + parts_ref[i * size : (i + 1) * size].astype(jnp.float32)
    hidden = hidden + attn
    hidden_ref[...] = hidden
    mean_square = jnp.mean(hidden * hidden, axis=-1, keepdims=True)
    normed = (hidden * lax.rsqrt(mean_square + 1e-06) * gain_ref[...]).astype(jnp.bfloat16)
    ids, codes = ids_ref[...], codes_ref[...]
    lane = lax.broadcasted_iota(jnp.int32, (size, LANES), 1)
    table = jnp.zeros((size, LANES), jnp.int32)
    for k in range(ids.shape[1]):
        code = codes[:, k : k + 1]
        table = table + jnp.where((lane == ids[:, k : k + 1]) | (lane == EXPERTS), code, 0)
    table = table.astype(jnp.float32).astype(jnp.bfloat16)
    for i in range(count):
        rows_ref[i * size : (i + 1) * size, :width] = normed
        rows_ref[i * size : (i + 1) * size, width:] = table


def normalize(parts, residual, gain, ids, codes, count):
    size, width = residual.shape
    return pl.pallas_call(
        functools.partial(norm_kernel, count),
        out_shape=[
            jax.ShapeDtypeStruct((size, width), jnp.float32),
            jax.ShapeDtypeStruct((count * size, width + LANES), jnp.bfloat16),
        ],
        in_specs=[vmem_spec()] * 5,
        out_specs=[vmem_spec()] * 2,
        compiler_params=pltpu.CompilerParams(vmem_limit_bytes=GRANT),
        cost_estimate=pl.CostEstimate(
            flops=20 * size * width, bytes_accessed=6 * count * size * width, transcendentals=size
        ),
    )(parts, residual, gain, ids, codes)


def swap_over_tensor(value):
    return lax.all_to_all(value, "tensor", split_axis=0, concat_axis=0, tiled=True)


def shift(value, turn, step):
    pairs = []
    for half in range(lax.axis_size("dp")):
        for row in range(SIDE):
            for col in range(SIDE):
                if (half + turn) % 2:
                    to_row, to_col = (row + step) % SIDE, col
                else:
                    to_row, to_col = row, (col + step) % SIDE
                base = half * SIDE * SIDE
                pairs.append((base + row * SIDE + col, base + to_row * SIDE + to_col))
    return lax.ppermute(value, ("dp", "expert"), pairs)


def send_round(block, turn):
    return shift(block, turn, 1), shift(block, turn, -1)


def send_on(back, front, turn):
    half = back.shape[0] // 2
    return shift(back[:half], turn, 1), shift(front[half:], turn, -1)


def add(*values):
    total = values[0].astype(jnp.float32)
    for value in values[1:]:
        total = total + value.astype(jnp.float32)
    return total


def tie(values, others):
    tied = lax.optimization_barrier((*values, *others))
    return tied[: len(values)], tied[len(values) :]


def packing(tail, expert, slots):
    rows = tail.shape[0]
    named = jnp.where(tail.astype(jnp.float32) > 0.0, 1.0, 0.0).astype(jnp.bfloat16)
    square = (rows, rows)
    below = lax.broadcasted_iota(jnp.int32, square, 0) > lax.broadcasted_iota(jnp.int32, square, 1)
    before = jnp.dot(
        jnp.where(below, 1.0, 0.0).astype(jnp.bfloat16), named, preferred_element_type=jnp.float32
    ).astype(jnp.bfloat16)
    lane = lax.broadcasted_iota(jnp.int32, (8, tail.shape[1]), 1)
    pick = jnp.where(lane == expert, 1.0, 0.0).astype(jnp.bfloat16)
    both_last = (((1,), (1,)), ((), ()))
    is_named = lax.dot_general(pick, named, both_last, preferred_element_type=jnp.float32)
    place = lax.dot_general(pick, before, both_last, preferred_element_type=jnp.float32)
    slot = lax.broadcasted_iota(jnp.int32, (slots, rows), 0).astype(jnp.float32)
    fills = (slot == place[:1]) & (is_named[:1] > 0.5)
    return jnp.where(fills, 1.0, 0.0).astype(jnp.bfloat16)


def pack_kernel(me_ref, dp_ref, back_ref, front_ref, low_ref, high_ref, low_hot_ref, high_hot_ref):
    slots, width = low_ref.shape
    half = back_ref.shape[0] // 2
    me = me_ref[0]
    row, col = me // SIDE, me % SIDE
    first = dp_ref[0] == 0
    ahead = jnp.where(first, (row + 1) % SIDE * SIDE + col, row * SIDE + (col + 1) % SIDE)
    behind = jnp.where(
        first, (row + SIDE - 1) % SIDE * SIDE + col, row * SIDE + (col + SIDE - 1) % SIDE
    )
    tail = width - LANES
    low_hot = packing(back_ref[:half, tail:], ahead, slots)
    high_hot = packing(front_ref[half:, tail:], behind, slots)
    low_hot_ref[...] = low_hot
    high_hot_ref[...] = high_hot
    low_ref[...] = jnp.dot(
        low_hot, back_ref[:half, :], preferred_element_type=jnp.float32
    ).astype(jnp.bfloat16)
    high_ref[...] = jnp.dot(
        high_hot, front_ref[half:, :], preferred_element_type=jnp.float32
    ).astype(jnp.bfloat16)


def pack(me, dp, back, front):
    rows, width = back.shape
    half = rows // 2
    slots = half // TOP_TOKENS * CAP
    smem = pl.BlockSpec(memory_space=pltpu.SMEM)
    return pl.pallas_call(
        pack_kernel,
        out_shape=[jax.ShapeDtypeStruct((slots, width), jnp.bfloat16)] * 2
        + [jax.ShapeDtypeStruct((slots, half), jnp.bfloat16)] * 2,
        in_specs=[smem] * 2 + [vmem_spec()] * 2,
        out_specs=[vmem_spec()] * 4,
        compiler_params=pltpu.CompilerParams(vmem_limit_bytes=GRANT),
        cost_estimate=pl.CostEstimate(
            flops=2 * rows * slots * width, bytes_accessed=4 * rows * width, transcendentals=0
        ),
    )(me, dp, back, front)


def join_kernel(
    _, back_ref, front_ref, low_ref, high_ref, low_hot_ref, high_hot_ref, to_front_ref, to_back_ref
):
    half = back_ref.shape[0] // 2
    first = (((0,), (0,)), ((), ()))

    def unpacked(hot_ref, value_ref):
        return lax.dot_general(
            hot_ref[...], value_ref[...], first, preferred_element_type=jnp.float32
        )

    low = back_ref[:half, :].astype(jnp.float32) + unpacked(low_hot_ref, low_ref)
    high = front_ref[half:, :].astype(jnp.float32) + unpacked(high_hot_ref, high_ref)
    to_back_ref[:half, :] = low.astype(jnp.bfloat16)
    to_back_ref[half:, :] = back_ref[half:, :]
    to_front_ref[:half, :] = front_ref[:half, :]
    to_front_ref[half:, :] = high.astype(jnp.bfloat16)


def join(after, back, front, low, high, low_hot, high_hot):
    rows, width = back.shape
    return pl.pallas_call(
        join_kernel,
        out_shape=[jax.ShapeDtypeStruct((rows, width), jnp.bfloat16)] * 2,
        in_specs=[pl.BlockSpec(memory_space=pl.ANY)] + [vmem_spec()] * 6,
        out_specs=[vmem_spec()] * 2,
        compiler_params=pltpu.CompilerParams(vmem_limit_bytes=GRANT),
        cost_estimate=pl.CostEstimate(
            flops=2 * rows * low.shape[0] * width, bytes_accessed=10 * rows * width, transcendentals=0
        ),
    )(after, back, front, low, high, low_hot, high_hot)


def pair_kernel(own_ref, back_ref, front_ref, pair_ref, low_ref, high_ref):
    size, half = own_ref.shape[0], low_ref.shape[0]
    pair_ref[:size] = own_ref[...]
    pair_ref[size:] = back_ref[...]
    low_ref[...] = back_ref[:half]
    high_ref[...] = front_ref[half:]


def pair(own, back, front):
    size, width = own.shape
    shapes = [(2 * size, width), (size // 2, width), (size // 2, width)]
    return pl.pallas_call(
        pair_kernel,
        out_shape=[jax.ShapeDtypeStruct(shape, own.dtype) for shape in shapes],
        in_specs=[vmem_spec()] * 3,
        out_specs=[vmem_spec()] * 3,
        compiler_params=pltpu.CompilerParams(vmem_limit_bytes=GRANT),
        cost_estimate=pl.CostEstimate(flops=0, bytes_accessed=12 * size * width, transcendentals=0),
    )(own, back, front)


def expert_kernel(count, me_ref, _, *refs):
    blocks, (gate_ref, up_ref, down_ref), outs = refs[:count], refs[count : count + 3], refs[count + 3 :]
    width = gate_ref.shape[1]
    x = jnp.concatenate([block[:, :width] for block in blocks])
    tail = jnp.concatenate([block[:, width:] for block in blocks]).astype(jnp.float32)
    lane = lax.broadcasted_iota(jnp.int32, tail.shape, 1)
    code = jnp.sum(jnp.where(lane == me_ref[0], tail, 0.0), axis=1, keepdims=True)
    total = jnp.sum(jnp.where(lane == EXPERTS, tail, 0.0), axis=1, keepdims=True)
    both_last = (((1,), (1,)), ((), ()))
    gate_value = lax.dot_general(x, gate_ref[...], both_last, preferred_element_type=jnp.float32)
    up_value = lax.dot_general(x, up_ref[...], both_last, preferred_element_type=jnp.float32)
    activated = (jax.nn.silu(gate_value) * up_value).astype(jnp.bfloat16)
    scale = code / jnp.maximum(total, 1.0)
    size = outs[0].shape[0]
    for start in range(0, width, CHUNK):
        down = jnp.dot(
            activated, down_ref[:, start : start + CHUNK], preferred_element_type=jnp.float32
        )
        result = (down * scale).astype(jnp.bfloat16)
        for i, out in enumerate(outs):
            out[:, start : start + CHUNK] = result[i * size : (i + 1) * size]


def run_expert(me, after, blocks, w_gate, w_up, w_down):
    count, size = len(blocks), blocks[0].shape[0]
    units, width = w_gate.shape
    vmem = pl.BlockSpec(memory_space=pltpu.VMEM)
    return pl.pallas_call(
        functools.partial(expert_kernel, count),
        out_shape=[jax.ShapeDtypeStruct((size, width), jnp.bfloat16)] * count,
        in_specs=[pl.BlockSpec(memory_space=pltpu.SMEM), pl.BlockSpec(memory_space=pl.ANY)]
        + [vmem] * (count + 3),
        out_specs=[vmem] * count,
        compiler_params=pltpu.CompilerParams(vmem_limit_bytes=GRANT),
        cost_estimate=pl.CostEstimate(
            flops=6 * count * size * units * width,
            bytes_accessed=4 * count * size * width + 6 * units * width,
            transcendentals=count * size * units,
        ),
    )(me, after, *blocks, w_gate, w_up, w_down)


def on_device(
    attn_heads, out_proj, residual, norm_gain, expert_ids, weight_codes, w_gate, w_up, w_down
):
    tensor_count = lax.axis_size("tensor")
    who = jnp.reshape(lax.axis_index("expert"), (1,)).astype(jnp.int32)
    side = jnp.reshape(lax.axis_index("dp"), (1,)).astype(jnp.int32)
    (heads,), (who, side) = tie((attn_heads[0],), (who, side))
    partial = project(heads, out_proj)
    hidden, rows = normalize(
        swap_over_tensor(partial),
        residual[0],
        norm_gain[None],
        expert_ids[0],
        weight_codes[0],
        tensor_count,
    )
    group = swap_over_tensor(rows)
    tokens, model_width = partial.shape

    weights = (w_gate[0], w_up[0], w_down[0])

    def experts(*blocks, after):
        return run_expert(who, after, blocks, *weights)

    def both(ahead, behind, turn):
        return shift(ahead, turn, 1), shift(behind, turn, -1)

    back, front = send_round(group, 0)
    first, low, high = pair(group, back, front)
    first_near = send_round(first, 1)
    far = both(low, high, 0)
    first_own = experts(first, after=low)
    second = jnp.concatenate([front, *far])
    (second,), first_own = tie((second,), first_own)
    second_near = send_round(second, 1)
    second_own = experts(second, after=first_own[0])
    first_near, second_own = tie(first_near, second_own)
    low, high, *first_hot = pack(who, side, *first_near)
    first_far = both(low, high, 1)
    first_near_out = experts(*first_near, after=low)
    second_near, first_near_out = tie(second_near, first_near_out)
    low, high, *second_hot = pack(who, side, *second_near)
    second_far = both(low, high, 1)
    first_far_low, first_far_high = experts(*first_far, after=high)
    first_down = both(first_far_high, first_far_low, 1)[::-1]
    second_far_low, second_far_high = experts(*second_far, after=first_far_low)
    second_down = both(second_far_high, second_far_low, 1)[::-1]
    second_near_out = experts(*second_near, after=second_far_low)
    first_send = join(second_near_out[0], *first_near_out, *first_down, *first_hot)
    second_send = join(first_send[1], *second_near_out, *second_down, *second_hot)
    first_got = both(*first_send, 1)
    second_got = both(*second_send, 1)
    first_sum = add(*first_own, *first_got).astype(jnp.bfloat16)
    (first_sum,), second_own = tie((first_sum,), second_own)
    second_sum = add(*second_own, *second_got).astype(jnp.bfloat16)

    half = tokens // 2
    up, down = both(second_sum[tokens : tokens + half], second_sum[tokens + half :], 0)
    front, back = second_sum[:tokens], first_sum[tokens:]
    front = jnp.concatenate([add(front[:half], up).astype(jnp.bfloat16), front[half:]])
    back = jnp.concatenate([back[:half], add(back[half:], down).astype(jnp.bfloat16)])
    got = both(front, back, 0)
    mixed = add(first_sum[:tokens], *got).astype(jnp.bfloat16)
    parts = swap_over_tensor(mixed).reshape(tensor_count, -1, model_width)
    layer_out = (hidden + jnp.sum(parts.astype(jnp.float32), axis=0)).astype(jnp.bfloat16)
    return layer_out[None]


def solution(mesh):
    return jax.shard_map(
        on_device,
        mesh=mesh,
        in_specs=(
            P(("dp", "expert"), None, "tensor"),
            P("tensor", None),
            P(("dp", "expert"), "tensor", None),
            P(),
            P(("dp", "expert"), "tensor", None),
            P(("dp", "expert"), "tensor", None),
            P("expert", "tensor", None),
            P("expert", "tensor", None),
            P("expert", "tensor", None),
        ),
        out_specs=P(("dp", "expert"), "tensor", None),
        check_vma=False,
    )
```

```python
import functools

import jax
import jax.numpy as jnp
from jax import lax
from jax.experimental import pallas as pl
from jax.experimental.pallas import tpu as pltpu
from jax.sharding import PartitionSpec as P

EXPERTS = 16
TOP_TOKENS, CAP = 8, 6
SIDE = 4
LANES = 128
CHUNK = 1024
STRIPE = 512
GRANT = 8 << 20
STREAM = 62 << 20


def vmem_spec():
    return pl.BlockSpec(memory_space=pltpu.VMEM)


def project_kernel(heads_hbm, proj_hbm, out_ref, heads_ref, proj_ref, sems):
    count, _, size = proj_ref.shape
    copies = [pltpu.make_async_copy(heads_hbm, heads_ref, sems.at[count])]
    for i in range(count):
        columns = pl.ds(i * size, size)
        copies.append(
            pltpu.make_async_copy(proj_hbm.at[:, columns], proj_ref.at[i], sems.at[i])
        )
    for copy in copies:
        copy.start()
    copies[0].wait()
    heads = heads_ref[...]
    for i in range(count):
        copies[i + 1].wait()
        out_ref[:, i * size : (i + 1) * size] = jnp.dot(
            heads, proj_ref[i], preferred_element_type=jnp.float32
        ).astype(jnp.bfloat16)


def project(heads, proj):
    tokens, features = heads.shape
    width = proj.shape[1]
    count = width // STRIPE
    return pl.pallas_call(
        project_kernel,
        out_shape=jax.ShapeDtypeStruct((tokens, width), jnp.bfloat16),
        in_specs=[pl.BlockSpec(memory_space=pl.ANY)] * 2,
        out_specs=vmem_spec(),
        scratch_shapes=[
            pltpu.VMEM((tokens, features), jnp.bfloat16),
            pltpu.VMEM((count, features, STRIPE), jnp.bfloat16),
            pltpu.SemaphoreType.DMA((count + 1,)),
        ],
        compiler_params=pltpu.CompilerParams(vmem_limit_bytes=STREAM),
        cost_estimate=pl.CostEstimate(
            flops=2 * tokens * features * width,
            bytes_accessed=2 * features * width,
            transcendentals=0,
        ),
    )(heads, proj)


def norm_kernel(count, parts_ref, residual_ref, gain_ref, ids_ref, codes_ref, hidden_ref, rows_ref):
    size, width = residual_ref.shape
    hidden = residual_ref[...].astype(jnp.float32)
    attn = parts_ref[:size].astype(jnp.float32)
    for i in range(1, count):
        attn = attn + parts_ref[i * size : (i + 1) * size].astype(jnp.float32)
    hidden = hidden + attn
    hidden_ref[...] = hidden
    mean_square = jnp.mean(hidden * hidden, axis=-1, keepdims=True)
    normed = (hidden * lax.rsqrt(mean_square + 1e-06) * gain_ref[...]).astype(jnp.bfloat16)
    ids, codes = ids_ref[...], codes_ref[...]
    lane = lax.broadcasted_iota(jnp.int32, (size, LANES), 1)
    table = jnp.zeros((size, LANES), jnp.int32)
    for k in range(ids.shape[1]):
        code = codes[:, k : k + 1]
        table = table + jnp.where((lane == ids[:, k : k + 1]) | (lane == EXPERTS), code, 0)
    table = table.astype(jnp.float32).astype(jnp.bfloat16)
    for i in range(count):
        rows_ref[i * size : (i + 1) * size, :width] = normed
        rows_ref[i * size : (i + 1) * size, width:] = table


def normalize(parts, residual, gain, ids, codes, count):
    size, width = residual.shape
    return pl.pallas_call(
        functools.partial(norm_kernel, count),
        out_shape=[
            jax.ShapeDtypeStruct((size, width), jnp.float32),
            jax.ShapeDtypeStruct((count * size, width + LANES), jnp.bfloat16),
        ],
        in_specs=[vmem_spec()] * 5,
        out_specs=[vmem_spec()] * 2,
        compiler_params=pltpu.CompilerParams(vmem_limit_bytes=GRANT),
        cost_estimate=pl.CostEstimate(
            flops=20 * size * width, bytes_accessed=6 * count * size * width, transcendentals=size
        ),
    )(parts, residual, gain, ids, codes)


def swap_over_tensor(value):
    return lax.all_to_all(value, "tensor", split_axis=0, concat_axis=0, tiled=True)


def shift(value, turn, step):
    pairs = []
    for half in range(lax.axis_size("dp")):
        for row in range(SIDE):
            for col in range(SIDE):
                if (half + turn) % 2:
                    to_row, to_col = (row + step) % SIDE, col
                else:
                    to_row, to_col = row, (col + step) % SIDE
                base = half * SIDE * SIDE
                pairs.append((base + row * SIDE + col, base + to_row * SIDE + to_col))
    return lax.ppermute(value, ("dp", "expert"), pairs)


def send_round(block, turn):
    return shift(block, turn, 1), shift(block, turn, -1)


def send_on(back, front, turn):
    half = back.shape[0] // 2
    return shift(back[:half], turn, 1), shift(front[half:], turn, -1)


def add(*values):
    total = values[0].astype(jnp.float32)
    for value in values[1:]:
        total = total + value.astype(jnp.float32)
    return total


def tie(values, others):
    tied = lax.optimization_barrier((*values, *others))
    return tied[: len(values)], tied[len(values) :]


def packing(tail, expert, slots):
    rows = tail.shape[0]
    named = jnp.where(tail.astype(jnp.float32) > 0.0, 1.0, 0.0).astype(jnp.bfloat16)
    square = (rows, rows)
    below = lax.broadcasted_iota(jnp.int32, square, 0) > lax.broadcasted_iota(jnp.int32, square, 1)
    before = jnp.dot(
        jnp.where(below, 1.0, 0.0).astype(jnp.bfloat16), named, preferred_element_type=jnp.float32
    ).astype(jnp.bfloat16)
    lane = lax.broadcasted_iota(jnp.int32, (8, tail.shape[1]), 1)
    pick = jnp.where(lane == expert, 1.0, 0.0).astype(jnp.bfloat16)
    both_last = (((1,), (1,)), ((), ()))
    is_named = lax.dot_general(pick, named, both_last, preferred_element_type=jnp.float32)
    place = lax.dot_general(pick, before, both_last, preferred_element_type=jnp.float32)
    slot = lax.broadcasted_iota(jnp.int32, (slots, rows), 0).astype(jnp.float32)
    fills = (slot == place[:1]) & (is_named[:1] > 0.5)
    return jnp.where(fills, 1.0, 0.0).astype(jnp.bfloat16)


def pack_kernel(me_ref, dp_ref, back_ref, front_ref, low_ref, high_ref, low_hot_ref, high_hot_ref):
    slots, width = low_ref.shape
    half = back_ref.shape[0] // 2
    me = me_ref[0]
    row, col = me // SIDE, me % SIDE
    first = dp_ref[0] == 0
    ahead = jnp.where(first, (row + 1) % SIDE * SIDE + col, row * SIDE + (col + 1) % SIDE)
    behind = jnp.where(
        first, (row + SIDE - 1) % SIDE * SIDE + col, row * SIDE + (col + SIDE - 1) % SIDE
    )
    tail = width - LANES
    low_hot = packing(back_ref[:half, tail:], ahead, slots)
    high_hot = packing(front_ref[half:, tail:], behind, slots)
    low_hot_ref[...] = low_hot
    high_hot_ref[...] = high_hot
    low_ref[...] = jnp.dot(
        low_hot, back_ref[:half, :], preferred_element_type=jnp.float32
    ).astype(jnp.bfloat16)
    high_ref[...] = jnp.dot(
        high_hot, front_ref[half:, :], preferred_element_type=jnp.float32
    ).astype(jnp.bfloat16)


def pack(me, dp, back, front):
    rows, width = back.shape
    half = rows // 2
    slots = half // TOP_TOKENS * CAP
    smem = pl.BlockSpec(memory_space=pltpu.SMEM)
    return pl.pallas_call(
        pack_kernel,
        out_shape=[jax.ShapeDtypeStruct((slots, width), jnp.bfloat16)] * 2
        + [jax.ShapeDtypeStruct((slots, half), jnp.bfloat16)] * 2,
        in_specs=[smem] * 2 + [vmem_spec()] * 2,
        out_specs=[vmem_spec()] * 4,
        compiler_params=pltpu.CompilerParams(vmem_limit_bytes=GRANT),
        cost_estimate=pl.CostEstimate(
            flops=2 * rows * slots * width, bytes_accessed=4 * rows * width, transcendentals=0
        ),
    )(me, dp, back, front)


def join_kernel(
    _, back_ref, front_ref, low_ref, high_ref, low_hot_ref, high_hot_ref, to_front_ref, to_back_ref
):
    half = back_ref.shape[0] // 2
    first = (((0,), (0,)), ((), ()))

    def unpacked(hot_ref, value_ref):
        return lax.dot_general(
            hot_ref[...], value_ref[...], first, preferred_element_type=jnp.float32
        )

    low = back_ref[:half, :].astype(jnp.float32) + unpacked(low_hot_ref, low_ref)
    high = front_ref[half:, :].astype(jnp.float32) + unpacked(high_hot_ref, high_ref)
    to_back_ref[:half, :] = low.astype(jnp.bfloat16)
    to_back_ref[half:, :] = back_ref[half:, :]
    to_front_ref[:half, :] = front_ref[:half, :]
    to_front_ref[half:, :] = high.astype(jnp.bfloat16)


def join(after, back, front, low, high, low_hot, high_hot):
    rows, width = back.shape
    return pl.pallas_call(
        join_kernel,
        out_shape=[jax.ShapeDtypeStruct((rows, width), jnp.bfloat16)] * 2,
        in_specs=[pl.BlockSpec(memory_space=pl.ANY)] + [vmem_spec()] * 6,
        out_specs=[vmem_spec()] * 2,
        compiler_params=pltpu.CompilerParams(vmem_limit_bytes=GRANT),
        cost_estimate=pl.CostEstimate(
            flops=2 * rows * low.shape[0] * width, bytes_accessed=10 * rows * width, transcendentals=0
        ),
    )(after, back, front, low, high, low_hot, high_hot)


def total_kernel(own_ref, a_ref, b_ref, *outs):
    start = 0
    for out in outs:
        rows = pl.ds(start, out.shape[0])
        out[...] = add(own_ref[rows, :], a_ref[rows, :], b_ref[rows, :]).astype(jnp.bfloat16)
        start += out.shape[0]


def total(own, got, sizes):
    rows, width = own.shape
    return pl.pallas_call(
        total_kernel,
        out_shape=[jax.ShapeDtypeStruct((size, width), jnp.bfloat16) for size in sizes],
        in_specs=[vmem_spec()] * 3,
        out_specs=[vmem_spec()] * len(sizes),
        compiler_params=pltpu.CompilerParams(vmem_limit_bytes=GRANT),
        cost_estimate=pl.CostEstimate(
            flops=2 * rows * width, bytes_accessed=8 * rows * width, transcendentals=0
        ),
    )(own, *got)


def join_last_kernel(front_ref, back_ref, up_ref, down_ref, to_front_ref, to_back_ref):
    half = up_ref.shape[0]
    to_front_ref[:half, :] = add(front_ref[:half, :], up_ref[...]).astype(jnp.bfloat16)
    to_front_ref[half:, :] = front_ref[half:, :]
    to_back_ref[:half, :] = back_ref[:half, :]
    to_back_ref[half:, :] = add(back_ref[half:, :], down_ref[...]).astype(jnp.bfloat16)


def join_last(front, back, up, down):
    rows, width = front.shape
    return pl.pallas_call(
        join_last_kernel,
        out_shape=[jax.ShapeDtypeStruct((rows, width), jnp.bfloat16)] * 2,
        in_specs=[vmem_spec()] * 4,
        out_specs=[vmem_spec()] * 2,
        compiler_params=pltpu.CompilerParams(vmem_limit_bytes=GRANT),
        cost_estimate=pl.CostEstimate(
            flops=rows * width, bytes_accessed=10 * rows * width, transcendentals=0
        ),
    )(front, back, up, down)


def pair_kernel(own_ref, back_ref, front_ref, pair_ref, low_ref, high_ref):
    size, half = own_ref.shape[0], low_ref.shape[0]
    pair_ref[:size] = own_ref[...]
    pair_ref[size:] = back_ref[...]
    low_ref[...] = back_ref[:half]
    high_ref[...] = front_ref[half:]


def pair(own, back, front):
    size, width = own.shape
    shapes = [(2 * size, width), (size // 2, width), (size // 2, width)]
    return pl.pallas_call(
        pair_kernel,
        out_shape=[jax.ShapeDtypeStruct(shape, own.dtype) for shape in shapes],
        in_specs=[vmem_spec()] * 3,
        out_specs=[vmem_spec()] * 3,
        compiler_params=pltpu.CompilerParams(vmem_limit_bytes=GRANT),
        cost_estimate=pl.CostEstimate(flops=0, bytes_accessed=12 * size * width, transcendentals=0),
    )(own, back, front)


def expert_kernel(count, me_ref, _, *refs):
    blocks, (gate_ref, up_ref, down_ref), outs = refs[:count], refs[count : count + 3], refs[count + 3 :]
    width = gate_ref.shape[1]
    x = jnp.concatenate([block[:, :width] for block in blocks])
    tail = jnp.concatenate([block[:, width:] for block in blocks]).astype(jnp.float32)
    lane = lax.broadcasted_iota(jnp.int32, tail.shape, 1)
    code = jnp.sum(jnp.where(lane == me_ref[0], tail, 0.0), axis=1, keepdims=True)
    total = jnp.sum(jnp.where(lane == EXPERTS, tail, 0.0), axis=1, keepdims=True)
    both_last = (((1,), (1,)), ((), ()))
    gate_value = lax.dot_general(x, gate_ref[...], both_last, preferred_element_type=jnp.float32)
    up_value = lax.dot_general(x, up_ref[...], both_last, preferred_element_type=jnp.float32)
    activated = (jax.nn.silu(gate_value) * up_value).astype(jnp.bfloat16)
    scale = code / jnp.maximum(total, 1.0)
    size = outs[0].shape[0]
    for start in range(0, width, CHUNK):
        down = jnp.dot(
            activated, down_ref[:, start : start + CHUNK], preferred_element_type=jnp.float32
        )
        result = (down * scale).astype(jnp.bfloat16)
        for i, out in enumerate(outs):
            out[:, start : start + CHUNK] = result[i * size : (i + 1) * size]


def run_expert(me, after, blocks, w_gate, w_up, w_down):
    count, size = len(blocks), blocks[0].shape[0]
    units, width = w_gate.shape
    vmem = pl.BlockSpec(memory_space=pltpu.VMEM)
    return pl.pallas_call(
        functools.partial(expert_kernel, count),
        out_shape=[jax.ShapeDtypeStruct((size, width), jnp.bfloat16)] * count,
        in_specs=[pl.BlockSpec(memory_space=pltpu.SMEM), pl.BlockSpec(memory_space=pl.ANY)]
        + [vmem] * (count + 3),
        out_specs=[vmem] * count,
        compiler_params=pltpu.CompilerParams(vmem_limit_bytes=GRANT),
        cost_estimate=pl.CostEstimate(
            flops=6 * count * size * units * width,
            bytes_accessed=4 * count * size * width + 6 * units * width,
            transcendentals=count * size * units,
        ),
    )(me, after, *blocks, w_gate, w_up, w_down)


def on_device(
    attn_heads, out_proj, residual, norm_gain, expert_ids, weight_codes, w_gate, w_up, w_down
):
    tensor_count = lax.axis_size("tensor")
    who = jnp.reshape(lax.axis_index("expert"), (1,)).astype(jnp.int32)
    side = jnp.reshape(lax.axis_index("dp"), (1,)).astype(jnp.int32)
    (heads,), (who, side) = tie((attn_heads[0],), (who, side))
    partial = project(heads, out_proj)
    hidden, rows = normalize(
        swap_over_tensor(partial),
        residual[0],
        norm_gain[None],
        expert_ids[0],
        weight_codes[0],
        tensor_count,
    )
    group = swap_over_tensor(rows)
    tokens, model_width = partial.shape

    weights = (w_gate[0], w_up[0], w_down[0])

    def experts(*blocks, after):
        return run_expert(who, after, blocks, *weights)

    def both(ahead, behind, turn):
        return shift(ahead, turn, 1), shift(behind, turn, -1)

    back, front = send_round(group, 0)
    first, low, high = pair(group, back, front)
    first_near = send_round(first, 1)
    far = both(low, high, 0)
    first_own = experts(first, after=low)
    second = jnp.concatenate([front, *far])
    (second,), first_own = tie((second,), first_own)
    second_near = send_round(second, 1)
    second_own = experts(second, after=first_own[0])
    first_near, second_own = tie(first_near, second_own)
    low, high, *first_hot = pack(who, side, *first_near)
    first_far = both(low, high, 1)
    first_near_out = experts(*first_near, after=low)
    second_near, first_near_out = tie(second_near, first_near_out)
    low, high, *second_hot = pack(who, side, *second_near)
    second_far = both(low, high, 1)
    first_far_low, first_far_high = experts(*first_far, after=high)
    first_down = both(first_far_high, first_far_low, 1)[::-1]
    second_far_low, second_far_high = experts(*second_far, after=first_far_low)
    second_down = both(second_far_high, second_far_low, 1)[::-1]
    second_near_out = experts(*second_near, after=second_far_low)
    first_down, second_down = tie(first_down, second_down)
    first_send = join(second_near_out[0], *first_near_out, *first_down, *first_hot)
    second_send = join(first_send[1], *second_near_out, *second_down, *second_hot)
    first_got = both(*first_send, 1)
    second_got = both(*second_send, 1)
    own, back = total(first_own[0], first_got, (tokens, tokens))
    half = tokens // 2
    front, low, high = total(second_own[0], second_got, (tokens, half, half))
    got = both(*join_last(front, back, *both(low, high, 0)), 0)
    mixed = add(own, *got).astype(jnp.bfloat16)
    parts = swap_over_tensor(mixed).reshape(tensor_count, -1, model_width)
    layer_out = (hidden + jnp.sum(parts.astype(jnp.float32), axis=0)).astype(jnp.bfloat16)
    return layer_out[None]


def solution(mesh):
    return jax.shard_map(
        on_device,
        mesh=mesh,
        in_specs=(
            P(("dp", "expert"), None, "tensor"),
            P("tensor", None),
            P(("dp", "expert"), "tensor", None),
            P(),
            P(("dp", "expert"), "tensor", None),
            P(("dp", "expert"), "tensor", None),
            P("expert", "tensor", None),
            P("expert", "tensor", None),
            P("expert", "tensor", None),
        ),
        out_specs=P(("dp", "expert"), "tensor", None),
        check_vma=False,
    )
```

```python
import functools

import jax
import jax.numpy as jnp
from jax import lax
from jax.experimental import pallas as pl
from jax.experimental.pallas import tpu as pltpu
from jax.sharding import PartitionSpec as P

EXPERTS = 16
TOP_TOKENS, CAP = 8, 6
SIDE = 4
LANES = 128
CHUNK = 1024
STRIPE = 512
GRANT = 8 << 20
STREAM = 62 << 20


def vmem_spec():
    return pl.BlockSpec(memory_space=pltpu.VMEM)


def project_kernel(heads_hbm, proj_hbm, out_ref, heads_ref, proj_ref, sems):
    count, _, size = proj_ref.shape
    copies = [pltpu.make_async_copy(heads_hbm, heads_ref, sems.at[count])]
    for i in range(count):
        columns = pl.ds(i * size, size)
        copies.append(
            pltpu.make_async_copy(proj_hbm.at[:, columns], proj_ref.at[i], sems.at[i])
        )
    for copy in copies:
        copy.start()
    copies[0].wait()
    heads = heads_ref[...]
    for i in range(count):
        copies[i + 1].wait()
        out_ref[:, i * size : (i + 1) * size] = jnp.dot(
            heads, proj_ref[i], preferred_element_type=jnp.float32
        ).astype(jnp.bfloat16)


def project(heads, proj):
    tokens, features = heads.shape
    width = proj.shape[1]
    count = width // STRIPE
    return pl.pallas_call(
        project_kernel,
        out_shape=jax.ShapeDtypeStruct((tokens, width), jnp.bfloat16),
        in_specs=[pl.BlockSpec(memory_space=pl.ANY)] * 2,
        out_specs=vmem_spec(),
        scratch_shapes=[
            pltpu.VMEM((tokens, features), jnp.bfloat16),
            pltpu.VMEM((count, features, STRIPE), jnp.bfloat16),
            pltpu.SemaphoreType.DMA((count + 1,)),
        ],
        compiler_params=pltpu.CompilerParams(vmem_limit_bytes=STREAM),
        cost_estimate=pl.CostEstimate(
            flops=2 * tokens * features * width,
            bytes_accessed=2 * features * width,
            transcendentals=0,
        ),
    )(heads, proj)


def norm_kernel(count, parts_ref, residual_ref, gain_ref, ids_ref, codes_ref, hidden_ref, rows_ref):
    size, width = residual_ref.shape
    hidden = residual_ref[...].astype(jnp.float32)
    attn = parts_ref[:size].astype(jnp.float32)
    for i in range(1, count):
        attn = attn + parts_ref[i * size : (i + 1) * size].astype(jnp.float32)
    hidden = hidden + attn
    hidden_ref[...] = hidden
    mean_square = jnp.mean(hidden * hidden, axis=-1, keepdims=True)
    normed = (hidden * lax.rsqrt(mean_square + 1e-06) * gain_ref[...]).astype(jnp.bfloat16)
    ids, codes = ids_ref[...], codes_ref[...]
    lane = lax.broadcasted_iota(jnp.int32, (size, LANES), 1)
    table = jnp.zeros((size, LANES), jnp.int32)
    for k in range(ids.shape[1]):
        code = codes[:, k : k + 1]
        table = table + jnp.where((lane == ids[:, k : k + 1]) | (lane == EXPERTS), code, 0)
    table = table.astype(jnp.float32).astype(jnp.bfloat16)
    for i in range(count):
        rows_ref[i * size : (i + 1) * size, :width] = normed
        rows_ref[i * size : (i + 1) * size, width:] = table


def normalize(parts, residual, gain, ids, codes, count):
    size, width = residual.shape
    return pl.pallas_call(
        functools.partial(norm_kernel, count),
        out_shape=[
            jax.ShapeDtypeStruct((size, width), jnp.float32),
            jax.ShapeDtypeStruct((count * size, width + LANES), jnp.bfloat16),
        ],
        in_specs=[vmem_spec()] * 5,
        out_specs=[vmem_spec()] * 2,
        compiler_params=pltpu.CompilerParams(vmem_limit_bytes=GRANT),
        cost_estimate=pl.CostEstimate(
            flops=20 * size * width, bytes_accessed=6 * count * size * width, transcendentals=size
        ),
    )(parts, residual, gain, ids, codes)


def swap_over_tensor(value):
    return lax.all_to_all(value, "tensor", split_axis=0, concat_axis=0, tiled=True)


def shift(value, turn, step):
    pairs = []
    for half in range(lax.axis_size("dp")):
        for row in range(SIDE):
            for col in range(SIDE):
                if (half + turn) % 2:
                    to_row, to_col = (row + step) % SIDE, col
                else:
                    to_row, to_col = row, (col + step) % SIDE
                base = half * SIDE * SIDE
                pairs.append((base + row * SIDE + col, base + to_row * SIDE + to_col))
    return lax.ppermute(value, ("dp", "expert"), pairs)


def add(*values):
    total = values[0].astype(jnp.float32)
    for value in values[1:]:
        total = total + value.astype(jnp.float32)
    return total


def tie(values, others):
    tied = lax.optimization_barrier((*values, *others))
    return tied[: len(values)], tied[len(values) :]


def packing(tail, expert, slots):
    rows = tail.shape[0]
    named = jnp.where(tail.astype(jnp.float32) > 0.0, 1.0, 0.0).astype(jnp.bfloat16)
    square = (rows, rows)
    below = lax.broadcasted_iota(jnp.int32, square, 0) > lax.broadcasted_iota(jnp.int32, square, 1)
    before = jnp.dot(
        jnp.where(below, 1.0, 0.0).astype(jnp.bfloat16), named, preferred_element_type=jnp.float32
    ).astype(jnp.bfloat16)
    lane = lax.broadcasted_iota(jnp.int32, (8, tail.shape[1]), 1)
    pick = jnp.where(lane == expert, 1.0, 0.0).astype(jnp.bfloat16)
    both_last = (((1,), (1,)), ((), ()))
    is_named = lax.dot_general(pick, named, both_last, preferred_element_type=jnp.float32)
    place = lax.dot_general(pick, before, both_last, preferred_element_type=jnp.float32)
    slot = lax.broadcasted_iota(jnp.int32, (slots, rows), 0).astype(jnp.float32)
    fills = (slot == place[:1]) & (is_named[:1] > 0.5)
    return jnp.where(fills, 1.0, 0.0).astype(jnp.bfloat16)


def beside(me_ref, dp_ref):
    row, col = me_ref[0] // SIDE, me_ref[0] % SIDE
    first = dp_ref[0] == 0
    ahead = jnp.where(first, (row + 1) % SIDE * SIDE + col, row * SIDE + (col + 1) % SIDE)
    back_row, back_col = (row + SIDE - 1) % SIDE, (col + SIDE - 1) % SIDE
    return ahead, jnp.where(first, back_row * SIDE + col, row * SIDE + back_col)


def chosen(hot, rows):
    return jnp.dot(hot, rows, preferred_element_type=jnp.float32).astype(jnp.bfloat16)


def unpacked(hot_ref, value):
    over_slots = (((0,), (0,)), ((), ()))
    return lax.dot_general(hot_ref[...], value, over_slots, preferred_element_type=jnp.float32)


def line_kernel(me_ref, dp_ref, _, low_ref, *refs):
    *highs, line_ref, to_ahead_ref, to_behind_ref, ahead_hot_ref, behind_hot_ref = refs
    slots, half = ahead_hot_ref.shape
    ahead, behind = beside(me_ref, dp_ref)
    tail = low_ref.shape[1] - LANES
    low, high = low_ref[...], jnp.concatenate([ref[...] for ref in highs])
    ahead_hot = packing(high[:, tail:], ahead, slots)
    behind_hot = packing(low[:, tail:], behind, slots)
    line_ref[:half, :] = low
    line_ref[half:, :] = high
    to_ahead_ref[:half, :] = low
    to_ahead_ref[half:, :] = chosen(ahead_hot, high)
    to_behind_ref[:slots, :] = chosen(behind_hot, low)
    to_behind_ref[slots:, :] = high
    ahead_hot_ref[...] = ahead_hot
    behind_hot_ref[...] = behind_hot


def make_line(me, dp, after, low, *highs):
    half, width = low.shape
    slots = half // TOP_TOKENS * CAP
    smem = pl.BlockSpec(memory_space=pltpu.SMEM)
    shapes = [(2 * half, width)] + [(half + slots, width)] * 2 + [(slots, half)] * 2
    return pl.pallas_call(
        line_kernel,
        out_shape=[jax.ShapeDtypeStruct(shape, jnp.bfloat16) for shape in shapes],
        in_specs=[smem] * 2 + [pl.BlockSpec(memory_space=pl.ANY)] + [vmem_spec()] * (1 + len(highs)),
        out_specs=[vmem_spec()] * 5,
        compiler_params=pltpu.CompilerParams(vmem_limit_bytes=GRANT),
        cost_estimate=pl.CostEstimate(
            flops=4 * half * slots * width, bytes_accessed=12 * half * width, transcendentals=0
        ),
    )(me, dp, after, low, *highs)


def pack_kernel(me_ref, dp_ref, back_ref, front_ref, low_ref, high_ref, low_hot_ref, high_hot_ref):
    slots, half = low_hot_ref.shape
    ahead, behind = beside(me_ref, dp_ref)
    tail = low_ref.shape[1] - LANES
    low_hot = packing(back_ref[:half, tail:], ahead, slots)
    high_hot = packing(front_ref[slots:, tail:], behind, slots)
    low_hot_ref[...] = low_hot
    high_hot_ref[...] = high_hot
    low_ref[...] = chosen(low_hot, back_ref[:half, :])
    high_ref[...] = chosen(high_hot, front_ref[slots:, :])


def pack(me, dp, half, back, front):
    rows, width = back.shape
    slots = rows - half
    smem = pl.BlockSpec(memory_space=pltpu.SMEM)
    return pl.pallas_call(
        pack_kernel,
        out_shape=[jax.ShapeDtypeStruct((slots, width), jnp.bfloat16)] * 2
        + [jax.ShapeDtypeStruct((slots, half), jnp.bfloat16)] * 2,
        in_specs=[smem] * 2 + [vmem_spec()] * 2,
        out_specs=[vmem_spec()] * 4,
        compiler_params=pltpu.CompilerParams(vmem_limit_bytes=GRANT),
        cost_estimate=pl.CostEstimate(
            flops=4 * half * slots * width, bytes_accessed=4 * rows * width, transcendentals=0
        ),
    )(me, dp, back, front)


def join_kernel(
    _, back_ref, front_ref, low_ref, high_ref, low_hot_ref, high_hot_ref, to_front_ref, to_back_ref
):
    slots, half = low_hot_ref.shape
    low = back_ref[:half, :].astype(jnp.float32) + unpacked(low_hot_ref, low_ref[...])
    high = front_ref[slots:, :].astype(jnp.float32) + unpacked(high_hot_ref, high_ref[...])
    to_back_ref[:half, :] = low.astype(jnp.bfloat16)
    to_back_ref[half:, :] = back_ref[half:, :]
    to_front_ref[:slots, :] = front_ref[:slots, :]
    to_front_ref[slots:, :] = high.astype(jnp.bfloat16)


def join(after, back, front, low, high, low_hot, high_hot):
    rows, width = back.shape
    return pl.pallas_call(
        join_kernel,
        out_shape=[jax.ShapeDtypeStruct((rows, width), jnp.bfloat16)] * 2,
        in_specs=[pl.BlockSpec(memory_space=pl.ANY)] + [vmem_spec()] * 6,
        out_specs=[vmem_spec()] * 2,
        compiler_params=pltpu.CompilerParams(vmem_limit_bytes=GRANT),
        cost_estimate=pl.CostEstimate(
            flops=2 * rows * low.shape[0] * width, bytes_accessed=10 * rows * width, transcendentals=0
        ),
    )(after, back, front, low, high, low_hot, high_hot)


def total_kernel(own_ref, back_ref, front_ref, ahead_hot_ref, behind_hot_ref, low_ref, *highs):
    slots, half = ahead_hot_ref.shape
    low = add(own_ref[:half, :], front_ref[:half, :]) + unpacked(behind_hot_ref, back_ref[:slots, :])
    low_ref[...] = low.astype(jnp.bfloat16)
    high = add(own_ref[half:, :], back_ref[slots:, :]) + unpacked(ahead_hot_ref, front_ref[half:, :])
    high = high.astype(jnp.bfloat16)
    size = highs[0].shape[0]
    for i, out in enumerate(highs):
        out[...] = high[i * size : (i + 1) * size]


def total(own, got, hots, sizes):
    rows, width = own.shape
    return pl.pallas_call(
        total_kernel,
        out_shape=[jax.ShapeDtypeStruct((size, width), jnp.bfloat16) for size in sizes],
        in_specs=[vmem_spec()] * 5,
        out_specs=[vmem_spec()] * len(sizes),
        compiler_params=pltpu.CompilerParams(vmem_limit_bytes=GRANT),
        cost_estimate=pl.CostEstimate(
            flops=2 * rows * width, bytes_accessed=8 * rows * width, transcendentals=0
        ),
    )(own, *got, *hots)


def join_last_kernel(front_ref, back_ref, up_ref, down_ref, to_front_ref, to_back_ref):
    half = up_ref.shape[0]
    to_front_ref[:half, :] = add(front_ref[:half, :], up_ref[...]).astype(jnp.bfloat16)
    to_front_ref[half:, :] = front_ref[half:, :]
    to_back_ref[:half, :] = back_ref[:half, :]
    to_back_ref[half:, :] = add(back_ref[half:, :], down_ref[...]).astype(jnp.bfloat16)


def join_last(front, back, up, down):
    rows, width = front.shape
    return pl.pallas_call(
        join_last_kernel,
        out_shape=[jax.ShapeDtypeStruct((rows, width), jnp.bfloat16)] * 2,
        in_specs=[vmem_spec()] * 4,
        out_specs=[vmem_spec()] * 2,
        compiler_params=pltpu.CompilerParams(vmem_limit_bytes=GRANT),
        cost_estimate=pl.CostEstimate(
            flops=rows * width, bytes_accessed=10 * rows * width, transcendentals=0
        ),
    )(front, back, up, down)


def expert_kernel(count, me_ref, _, *refs):
    blocks, (gate_ref, up_ref, down_ref), outs = refs[:count], refs[count : count + 3], refs[count + 3 :]
    width = gate_ref.shape[1]
    x = jnp.concatenate([block[:, :width] for block in blocks])
    tail = jnp.concatenate([block[:, width:] for block in blocks]).astype(jnp.float32)
    lane = lax.broadcasted_iota(jnp.int32, tail.shape, 1)
    code = jnp.sum(jnp.where(lane == me_ref[0], tail, 0.0), axis=1, keepdims=True)
    total = jnp.sum(jnp.where(lane == EXPERTS, tail, 0.0), axis=1, keepdims=True)
    both_last = (((1,), (1,)), ((), ()))
    gate_value = lax.dot_general(x, gate_ref[...], both_last, preferred_element_type=jnp.float32)
    up_value = lax.dot_general(x, up_ref[...], both_last, preferred_element_type=jnp.float32)
    activated = (jax.nn.silu(gate_value) * up_value).astype(jnp.bfloat16)
    scale = code / jnp.maximum(total, 1.0)
    size = outs[0].shape[0]
    for start in range(0, width, CHUNK):
        down = jnp.dot(
            activated, down_ref[:, start : start + CHUNK], preferred_element_type=jnp.float32
        )
        result = (down * scale).astype(jnp.bfloat16)
        for i, out in enumerate(outs):
            out[:, start : start + CHUNK] = result[i * size : (i + 1) * size]


def run_expert(me, after, blocks, w_gate, w_up, w_down):
    count, size = len(blocks), blocks[0].shape[0]
    units, width = w_gate.shape
    vmem = pl.BlockSpec(memory_space=pltpu.VMEM)
    return pl.pallas_call(
        functools.partial(expert_kernel, count),
        out_shape=[jax.ShapeDtypeStruct((size, width), jnp.bfloat16)] * count,
        in_specs=[pl.BlockSpec(memory_space=pltpu.SMEM), pl.BlockSpec(memory_space=pl.ANY)]
        + [vmem] * (count + 3),
        out_specs=[vmem] * count,
        compiler_params=pltpu.CompilerParams(vmem_limit_bytes=GRANT),
        cost_estimate=pl.CostEstimate(
            flops=6 * count * size * units * width,
            bytes_accessed=4 * count * size * width + 6 * units * width,
            transcendentals=count * size * units,
        ),
    )(me, after, *blocks, w_gate, w_up, w_down)


def on_device(
    attn_heads, out_proj, residual, norm_gain, expert_ids, weight_codes, w_gate, w_up, w_down
):
    tensor_count = lax.axis_size("tensor")
    who = jnp.reshape(lax.axis_index("expert"), (1,)).astype(jnp.int32)
    side = jnp.reshape(lax.axis_index("dp"), (1,)).astype(jnp.int32)
    (heads,), (who, side) = tie((attn_heads[0],), (who, side))
    partial = project(heads, out_proj)
    hidden, rows = normalize(
        swap_over_tensor(partial),
        residual[0],
        norm_gain[None],
        expert_ids[0],
        weight_codes[0],
        tensor_count,
    )
    group = swap_over_tensor(rows)
    tokens, model_width = partial.shape

    weights = (w_gate[0], w_up[0], w_down[0])

    def experts(*blocks, after):
        return run_expert(who, after, blocks, *weights)

    def both(ahead, behind, turn):
        return shift(ahead, turn, 1), shift(behind, turn, -1)

    half = tokens // 2
    back, front = both(group, group, 0)
    first, *first_sent, first_ahead, first_behind = make_line(who, side, front, group, back)
    first_near = both(*first_sent, 1)
    far = both(back[:half], front[half:], 0)
    first_own = experts(first, after=back)
    second, *second_sent, second_ahead, second_behind = make_line(
        who, side, first_own[0], front, *far
    )
    second_near = both(*second_sent, 1)
    second_own = experts(second, after=first_own[0])
    first_near, second_own = tie(first_near, second_own)
    low, high, *first_hot = pack(who, side, tokens, *first_near)
    first_far = both(low, high, 1)
    first_near_out = experts(*first_near, after=low)
    second_near, first_near_out = tie(second_near, first_near_out)
    low, high, *second_hot = pack(who, side, tokens, *second_near)
    second_far = both(low, high, 1)
    first_far_low, first_far_high = experts(*first_far, after=high)
    first_down = both(first_far_high, first_far_low, 1)[::-1]
    second_far_low, second_far_high = experts(*second_far, after=first_far_low)
    second_down = both(second_far_high, second_far_low, 1)[::-1]
    second_near_out = experts(*second_near, after=second_far_low)
    first_down, second_down = tie(first_down, second_down)
    first_send = join(second_near_out[0], *first_near_out, *first_down, *first_hot)
    second_send = join(first_send[1], *second_near_out, *second_down, *second_hot)
    first_got = both(*first_send, 1)
    second_got = both(*second_send, 1)
    own, back = total(first_own[0], first_got, (first_ahead, first_behind), (tokens, tokens))
    hots = (second_ahead, second_behind)
    front, low, high = total(second_own[0], second_got, hots, (tokens, half, half))
    got = both(*join_last(front, back, *both(low, high, 0)), 0)
    mixed = add(own, *got).astype(jnp.bfloat16)
    parts = swap_over_tensor(mixed).reshape(tensor_count, -1, model_width)
    layer_out = (hidden + jnp.sum(parts.astype(jnp.float32), axis=0)).astype(jnp.bfloat16)
    return layer_out[None]


def solution(mesh):
    return jax.shard_map(
        on_device,
        mesh=mesh,
        in_specs=(
            P(("dp", "expert"), None, "tensor"),
            P("tensor", None),
            P(("dp", "expert"), "tensor", None),
            P(),
            P(("dp", "expert"), "tensor", None),
            P(("dp", "expert"), "tensor", None),
            P("expert", "tensor", None),
            P("expert", "tensor", None),
            P("expert", "tensor", None),
        ),
        out_specs=P(("dp", "expert"), "tensor", None),
        check_vma=False,
    )
```

```python
import functools

import jax
import jax.numpy as jnp
from jax import lax
from jax.experimental import pallas as pl
from jax.experimental.pallas import tpu as pltpu
from jax.sharding import PartitionSpec as P

EXPERTS = 16
TOP_TOKENS, CAP = 8, 6
SIDE = 4
LANES = 128
CHUNK = 1024
STRIPE = 512
GRANT = 8 << 20
STREAM = 62 << 20


def vmem_spec():
    return pl.BlockSpec(memory_space=pltpu.VMEM)


def project_kernel(heads_hbm, proj_hbm, out_ref, heads_ref, proj_ref, sems):
    count, _, size = proj_ref.shape
    copies = [pltpu.make_async_copy(heads_hbm, heads_ref, sems.at[count])]
    for i in range(count):
        columns = pl.ds(i * size, size)
        copies.append(
            pltpu.make_async_copy(proj_hbm.at[:, columns], proj_ref.at[i], sems.at[i])
        )
    for copy in copies:
        copy.start()
    copies[0].wait()
    heads = heads_ref[...]
    for i in range(count):
        copies[i + 1].wait()
        out_ref[:, i * size : (i + 1) * size] = jnp.dot(
            heads, proj_ref[i], preferred_element_type=jnp.float32
        ).astype(jnp.bfloat16)


def project(heads, proj):
    tokens, features = heads.shape
    width = proj.shape[1]
    count = width // STRIPE
    return pl.pallas_call(
        project_kernel,
        out_shape=jax.ShapeDtypeStruct((tokens, width), jnp.bfloat16),
        in_specs=[pl.BlockSpec(memory_space=pl.ANY)] * 2,
        out_specs=vmem_spec(),
        scratch_shapes=[
            pltpu.VMEM((tokens, features), jnp.bfloat16),
            pltpu.VMEM((count, features, STRIPE), jnp.bfloat16),
            pltpu.SemaphoreType.DMA((count + 1,)),
        ],
        compiler_params=pltpu.CompilerParams(vmem_limit_bytes=STREAM),
        cost_estimate=pl.CostEstimate(
            flops=2 * tokens * features * width,
            bytes_accessed=2 * features * width,
            transcendentals=0,
        ),
    )(heads, proj)


def norm_kernel(count, parts_ref, residual_ref, gain_ref, ids_ref, codes_ref, hidden_ref, rows_ref):
    size, width = residual_ref.shape
    hidden = residual_ref[...].astype(jnp.float32)
    attn = parts_ref[:size].astype(jnp.float32)
    for i in range(1, count):
        attn = attn + parts_ref[i * size : (i + 1) * size].astype(jnp.float32)
    hidden = hidden + attn
    hidden_ref[...] = hidden
    mean_square = jnp.mean(hidden * hidden, axis=-1, keepdims=True)
    normed = (hidden * lax.rsqrt(mean_square + 1e-06) * gain_ref[...]).astype(jnp.bfloat16)
    ids, codes = ids_ref[...], codes_ref[...]
    lane = lax.broadcasted_iota(jnp.int32, (size, LANES), 1)
    table = jnp.zeros((size, LANES), jnp.int32)
    for k in range(ids.shape[1]):
        code = codes[:, k : k + 1]
        table = table + jnp.where((lane == ids[:, k : k + 1]) | (lane == EXPERTS), code, 0)
    table = table.astype(jnp.float32).astype(jnp.bfloat16)
    for i in range(count):
        rows_ref[i * size : (i + 1) * size, :width] = normed
        rows_ref[i * size : (i + 1) * size, width:] = table


def normalize(parts, residual, gain, ids, codes, count):
    size, width = residual.shape
    return pl.pallas_call(
        functools.partial(norm_kernel, count),
        out_shape=[
            jax.ShapeDtypeStruct((size, width), jnp.float32),
            jax.ShapeDtypeStruct((count * size, width + LANES), jnp.bfloat16),
        ],
        in_specs=[vmem_spec()] * 5,
        out_specs=[vmem_spec()] * 2,
        compiler_params=pltpu.CompilerParams(vmem_limit_bytes=GRANT),
        cost_estimate=pl.CostEstimate(
            flops=20 * size * width, bytes_accessed=6 * count * size * width, transcendentals=size
        ),
    )(parts, residual, gain, ids, codes)


def swap_over_tensor(value):
    return lax.all_to_all(value, "tensor", split_axis=0, concat_axis=0, tiled=True)


def shift(value, turn, step):
    pairs = []
    for half in range(lax.axis_size("dp")):
        for row in range(SIDE):
            for col in range(SIDE):
                if (half + turn) % 2:
                    to_row, to_col = (row + step) % SIDE, col
                else:
                    to_row, to_col = row, (col + step) % SIDE
                base = half * SIDE * SIDE
                pairs.append((base + row * SIDE + col, base + to_row * SIDE + to_col))
    return lax.ppermute(value, ("dp", "expert"), pairs)


def add(*values):
    total = values[0].astype(jnp.float32)
    for value in values[1:]:
        total = total + value.astype(jnp.float32)
    return total


def tie(values, others):
    tied = lax.optimization_barrier((*values, *others))
    return tied[: len(values)], tied[len(values) :]


def packing(tail, expert, slots):
    rows = tail.shape[0]
    named = jnp.where(tail.astype(jnp.float32) > 0.0, 1.0, 0.0).astype(jnp.bfloat16)
    square = (rows, rows)
    below = lax.broadcasted_iota(jnp.int32, square, 0) > lax.broadcasted_iota(jnp.int32, square, 1)
    before = jnp.dot(
        jnp.where(below, 1.0, 0.0).astype(jnp.bfloat16), named, preferred_element_type=jnp.float32
    ).astype(jnp.bfloat16)
    lane = lax.broadcasted_iota(jnp.int32, (8, tail.shape[1]), 1)
    pick = jnp.where(lane == expert, 1.0, 0.0).astype(jnp.bfloat16)
    both_last = (((1,), (1,)), ((), ()))
    is_named = lax.dot_general(pick, named, both_last, preferred_element_type=jnp.float32)
    place = lax.dot_general(pick, before, both_last, preferred_element_type=jnp.float32)
    slot = lax.broadcasted_iota(jnp.int32, (slots, rows), 0).astype(jnp.float32)
    fills = (slot == place[:1]) & (is_named[:1] > 0.5)
    return jnp.where(fills, 1.0, 0.0).astype(jnp.bfloat16)


def beside(me_ref, dp_ref):
    row, col = me_ref[0] // SIDE, me_ref[0] % SIDE
    first = dp_ref[0] == 0
    ahead = jnp.where(first, (row + 1) % SIDE * SIDE + col, row * SIDE + (col + 1) % SIDE)
    back_row, back_col = (row + SIDE - 1) % SIDE, (col + SIDE - 1) % SIDE
    return ahead, jnp.where(first, back_row * SIDE + col, row * SIDE + back_col)


def chosen(hot, rows):
    return jnp.dot(hot, rows, preferred_element_type=jnp.float32).astype(jnp.bfloat16)


def unpacked(hot_ref, value):
    over_slots = (((0,), (0,)), ((), ()))
    return lax.dot_general(hot_ref[...], value, over_slots, preferred_element_type=jnp.float32)


def line_kernel(me_ref, dp_ref, _, low_ref, *refs):
    *highs, line_ref, to_ahead_ref, to_behind_ref, ahead_hot_ref, behind_hot_ref = refs
    slots, half = ahead_hot_ref.shape
    ahead, behind = beside(me_ref, dp_ref)
    tail = low_ref.shape[1] - LANES
    low, high = low_ref[...], jnp.concatenate([ref[...] for ref in highs])
    ahead_hot = packing(high[:, tail:], ahead, slots)
    behind_hot = packing(low[:, tail:], behind, slots)
    line_ref[:half, :] = low
    line_ref[half:, :] = high
    to_ahead_ref[:half, :] = low
    to_ahead_ref[half:, :] = chosen(ahead_hot, high)
    to_behind_ref[:slots, :] = chosen(behind_hot, low)
    to_behind_ref[slots:, :] = high
    ahead_hot_ref[...] = ahead_hot
    behind_hot_ref[...] = behind_hot


def make_line(me, dp, after, low, *highs):
    half, width = low.shape
    slots = half // TOP_TOKENS * CAP
    smem = pl.BlockSpec(memory_space=pltpu.SMEM)
    shapes = [(2 * half, width)] + [(half + slots, width)] * 2 + [(slots, half)] * 2
    return pl.pallas_call(
        line_kernel,
        out_shape=[jax.ShapeDtypeStruct(shape, jnp.bfloat16) for shape in shapes],
        in_specs=[smem] * 2 + [pl.BlockSpec(memory_space=pl.ANY)] + [vmem_spec()] * (1 + len(highs)),
        out_specs=[vmem_spec()] * 5,
        compiler_params=pltpu.CompilerParams(vmem_limit_bytes=GRANT),
        cost_estimate=pl.CostEstimate(
            flops=4 * half * slots * width, bytes_accessed=12 * half * width, transcendentals=0
        ),
    )(me, dp, after, low, *highs)


def pack_kernel(
    me_ref, dp_ref, _, back_ref, front_ref, low_ref, high_ref, low_hot_ref, high_hot_ref
):
    slots, half = low_hot_ref.shape
    ahead, behind = beside(me_ref, dp_ref)
    tail = low_ref.shape[1] - LANES
    low_hot = packing(back_ref[:half, tail:], ahead, slots)
    high_hot = packing(front_ref[slots:, tail:], behind, slots)
    low_hot_ref[...] = low_hot
    high_hot_ref[...] = high_hot
    low_ref[...] = chosen(low_hot, back_ref[:half, :])
    high_ref[...] = chosen(high_hot, front_ref[slots:, :])


def pack(me, dp, half, after, back, front):
    rows, width = back.shape
    slots = rows - half
    smem = pl.BlockSpec(memory_space=pltpu.SMEM)
    return pl.pallas_call(
        pack_kernel,
        out_shape=[jax.ShapeDtypeStruct((slots, width), jnp.bfloat16)] * 2
        + [jax.ShapeDtypeStruct((slots, half), jnp.bfloat16)] * 2,
        in_specs=[smem] * 2 + [pl.BlockSpec(memory_space=pl.ANY)] + [vmem_spec()] * 2,
        out_specs=[vmem_spec()] * 4,
        compiler_params=pltpu.CompilerParams(vmem_limit_bytes=GRANT),
        cost_estimate=pl.CostEstimate(
            flops=4 * half * slots * width, bytes_accessed=4 * rows * width, transcendentals=0
        ),
    )(me, dp, after, back, front)


def join_kernel(
    _, back_ref, front_ref, low_ref, high_ref, low_hot_ref, high_hot_ref, to_front_ref, to_back_ref
):
    slots, half = low_hot_ref.shape
    low = back_ref[:half, :].astype(jnp.float32) + unpacked(low_hot_ref, low_ref[...])
    high = front_ref[slots:, :].astype(jnp.float32) + unpacked(high_hot_ref, high_ref[...])
    to_back_ref[:half, :] = low.astype(jnp.bfloat16)
    to_back_ref[half:, :] = back_ref[half:, :]
    to_front_ref[:slots, :] = front_ref[:slots, :]
    to_front_ref[slots:, :] = high.astype(jnp.bfloat16)


def join(after, back, front, low, high, low_hot, high_hot):
    rows, width = back.shape
    return pl.pallas_call(
        join_kernel,
        out_shape=[jax.ShapeDtypeStruct((rows, width), jnp.bfloat16)] * 2,
        in_specs=[pl.BlockSpec(memory_space=pl.ANY)] + [vmem_spec()] * 6,
        out_specs=[vmem_spec()] * 2,
        compiler_params=pltpu.CompilerParams(vmem_limit_bytes=GRANT),
        cost_estimate=pl.CostEstimate(
            flops=2 * rows * low.shape[0] * width, bytes_accessed=10 * rows * width, transcendentals=0
        ),
    )(after, back, front, low, high, low_hot, high_hot)


def total_kernel(own_ref, back_ref, front_ref, ahead_hot_ref, behind_hot_ref, low_ref, *highs):
    slots, half = ahead_hot_ref.shape
    low = add(own_ref[:half, :], front_ref[:half, :]) + unpacked(behind_hot_ref, back_ref[:slots, :])
    low_ref[...] = low.astype(jnp.bfloat16)
    high = add(own_ref[half:, :], back_ref[slots:, :]) + unpacked(ahead_hot_ref, front_ref[half:, :])
    high = high.astype(jnp.bfloat16)
    size = highs[0].shape[0]
    for i, out in enumerate(highs):
        out[...] = high[i * size : (i + 1) * size]


def total(own, got, hots, sizes):
    rows, width = own.shape
    return pl.pallas_call(
        total_kernel,
        out_shape=[jax.ShapeDtypeStruct((size, width), jnp.bfloat16) for size in sizes],
        in_specs=[vmem_spec()] * 5,
        out_specs=[vmem_spec()] * len(sizes),
        compiler_params=pltpu.CompilerParams(vmem_limit_bytes=GRANT),
        cost_estimate=pl.CostEstimate(
            flops=2 * rows * width, bytes_accessed=8 * rows * width, transcendentals=0
        ),
    )(own, *got, *hots)


def join_last_kernel(front_ref, back_ref, up_ref, down_ref, to_front_ref, to_back_ref):
    half = up_ref.shape[0]
    to_front_ref[:half, :] = add(front_ref[:half, :], up_ref[...]).astype(jnp.bfloat16)
    to_front_ref[half:, :] = front_ref[half:, :]
    to_back_ref[:half, :] = back_ref[:half, :]
    to_back_ref[half:, :] = add(back_ref[half:, :], down_ref[...]).astype(jnp.bfloat16)


def join_last(front, back, up, down):
    rows, width = front.shape
    return pl.pallas_call(
        join_last_kernel,
        out_shape=[jax.ShapeDtypeStruct((rows, width), jnp.bfloat16)] * 2,
        in_specs=[vmem_spec()] * 4,
        out_specs=[vmem_spec()] * 2,
        compiler_params=pltpu.CompilerParams(vmem_limit_bytes=GRANT),
        cost_estimate=pl.CostEstimate(
            flops=rows * width, bytes_accessed=10 * rows * width, transcendentals=0
        ),
    )(front, back, up, down)


def expert_kernel(count, me_ref, _, *refs):
    blocks, (gate_ref, up_ref, down_ref), outs = refs[:count], refs[count : count + 3], refs[count + 3 :]
    width = gate_ref.shape[1]
    x = jnp.concatenate([block[:, :width] for block in blocks])
    tail = jnp.concatenate([block[:, width:] for block in blocks]).astype(jnp.float32)
    lane = lax.broadcasted_iota(jnp.int32, tail.shape, 1)
    code = jnp.sum(jnp.where(lane == me_ref[0], tail, 0.0), axis=1, keepdims=True)
    total = jnp.sum(jnp.where(lane == EXPERTS, tail, 0.0), axis=1, keepdims=True)
    both_last = (((1,), (1,)), ((), ()))
    gate_value = lax.dot_general(x, gate_ref[...], both_last, preferred_element_type=jnp.float32)
    up_value = lax.dot_general(x, up_ref[...], both_last, preferred_element_type=jnp.float32)
    activated = (jax.nn.silu(gate_value) * up_value).astype(jnp.bfloat16)
    scale = code / jnp.maximum(total, 1.0)
    size = outs[0].shape[0]
    for start in range(0, width, CHUNK):
        down = jnp.dot(
            activated, down_ref[:, start : start + CHUNK], preferred_element_type=jnp.float32
        )
        result = (down * scale).astype(jnp.bfloat16)
        for i, out in enumerate(outs):
            out[:, start : start + CHUNK] = result[i * size : (i + 1) * size]


def run_expert(me, after, blocks, w_gate, w_up, w_down):
    count, size = len(blocks), blocks[0].shape[0]
    units, width = w_gate.shape
    vmem = pl.BlockSpec(memory_space=pltpu.VMEM)
    return pl.pallas_call(
        functools.partial(expert_kernel, count),
        out_shape=[jax.ShapeDtypeStruct((size, width), jnp.bfloat16)] * count,
        in_specs=[pl.BlockSpec(memory_space=pltpu.SMEM), pl.BlockSpec(memory_space=pl.ANY)]
        + [vmem] * (count + 3),
        out_specs=[vmem] * count,
        compiler_params=pltpu.CompilerParams(vmem_limit_bytes=GRANT),
        cost_estimate=pl.CostEstimate(
            flops=6 * count * size * units * width,
            bytes_accessed=4 * count * size * width + 6 * units * width,
            transcendentals=count * size * units,
        ),
    )(me, after, *blocks, w_gate, w_up, w_down)


def on_device(
    attn_heads, out_proj, residual, norm_gain, expert_ids, weight_codes, w_gate, w_up, w_down
):
    tensor_count = lax.axis_size("tensor")
    who = jnp.reshape(lax.axis_index("expert"), (1,)).astype(jnp.int32)
    side = jnp.reshape(lax.axis_index("dp"), (1,)).astype(jnp.int32)
    (heads,), (who, side) = tie((attn_heads[0],), (who, side))
    partial = project(heads, out_proj)
    hidden, rows = normalize(
        swap_over_tensor(partial),
        residual[0],
        norm_gain[None],
        expert_ids[0],
        weight_codes[0],
        tensor_count,
    )
    group = swap_over_tensor(rows)
    tokens, model_width = partial.shape

    weights = (w_gate[0], w_up[0], w_down[0])

    def experts(*blocks, after):
        return run_expert(who, after, blocks, *weights)

    def both(ahead, behind, turn):
        return shift(ahead, turn, 1), shift(behind, turn, -1)

    half = tokens // 2
    back, front = both(group, group, 0)
    first, *first_sent, first_ahead, first_behind = make_line(who, side, front, group, back)
    first_near = both(*first_sent, 1)
    far = both(back[:half], front[half:], 0)
    first_own = experts(first, after=back)
    second, *second_sent, second_ahead, second_behind = make_line(
        who, side, first_own[0], front, *far
    )
    second_near = both(*second_sent, 1)
    first_near_out = experts(*first_near, after=first_own[0])
    second_own = experts(second, after=first_near_out[0])
    low, high, *first_hot = pack(who, side, tokens, second_own[0], *first_near)
    first_far = both(low, high, 1)
    second_near, first_near_out = tie(second_near, first_near_out)
    low, high, *second_hot = pack(who, side, tokens, low, *second_near)
    second_far = both(low, high, 1)
    first_far_low, first_far_high = experts(*first_far, after=high)
    first_down = both(first_far_high, first_far_low, 1)[::-1]
    second_far_low, second_far_high = experts(*second_far, after=first_far_low)
    second_down = both(second_far_high, second_far_low, 1)[::-1]
    second_near_out = experts(*second_near, after=second_far_low)
    first_down, second_down = tie(first_down, second_down)
    first_send = join(second_near_out[0], *first_near_out, *first_down, *first_hot)
    second_send = join(first_send[1], *second_near_out, *second_down, *second_hot)
    first_got = both(*first_send, 1)
    second_got = both(*second_send, 1)
    own, back = total(first_own[0], first_got, (first_ahead, first_behind), (tokens, tokens))
    hots = (second_ahead, second_behind)
    front, low, high = total(second_own[0], second_got, hots, (tokens, half, half))
    got = both(*join_last(front, back, *both(low, high, 0)), 0)
    mixed = add(own, *got).astype(jnp.bfloat16)
    parts = swap_over_tensor(mixed).reshape(tensor_count, -1, model_width)
    layer_out = (hidden + jnp.sum(parts.astype(jnp.float32), axis=0)).astype(jnp.bfloat16)
    return layer_out[None]


def solution(mesh):
    return jax.shard_map(
        on_device,
        mesh=mesh,
        in_specs=(
            P(("dp", "expert"), None, "tensor"),
            P("tensor", None),
            P(("dp", "expert"), "tensor", None),
            P(),
            P(("dp", "expert"), "tensor", None),
            P(("dp", "expert"), "tensor", None),
            P("expert", "tensor", None),
            P("expert", "tensor", None),
            P("expert", "tensor", None),
        ),
        out_specs=P(("dp", "expert"), "tensor", None),
        check_vma=False,
    )
```

```python
import functools

import jax
import jax.numpy as jnp
from jax import lax
from jax.experimental import pallas as pl
from jax.experimental.pallas import tpu as pltpu
from jax.sharding import PartitionSpec as P

EXPERTS = 16
TOP_TOKENS, CAP = 8, 6
SIDE = 4
LANES = 128
CHUNK = 1024
STRIPE = 1024
GRANT = 8 << 20
STREAM = 62 << 20


def vmem_spec():
    return pl.BlockSpec(memory_space=pltpu.VMEM)


def project_kernel(heads_hbm, proj_hbm, out_ref, heads_ref, proj_ref, sems):
    count, _, size = proj_ref.shape
    copies = [pltpu.make_async_copy(heads_hbm, heads_ref, sems.at[count])]
    for i in range(count):
        columns = pl.ds(i * size, size)
        copies.append(
            pltpu.make_async_copy(proj_hbm.at[:, columns], proj_ref.at[i], sems.at[i])
        )
    for copy in copies:
        copy.start()
    copies[0].wait()
    heads = heads_ref[...]
    for i in range(count):
        copies[i + 1].wait()
        out_ref[:, i * size : (i + 1) * size] = jnp.dot(
            heads, proj_ref[i], preferred_element_type=jnp.float32
        ).astype(jnp.bfloat16)


def project(heads, proj):
    tokens, features = heads.shape
    width = proj.shape[1]
    count = width // STRIPE
    return pl.pallas_call(
        project_kernel,
        out_shape=jax.ShapeDtypeStruct((tokens, width), jnp.bfloat16),
        in_specs=[pl.BlockSpec(memory_space=pl.ANY)] * 2,
        out_specs=vmem_spec(),
        scratch_shapes=[
            pltpu.VMEM((tokens, features), jnp.bfloat16),
            pltpu.VMEM((count, features, STRIPE), jnp.bfloat16),
            pltpu.SemaphoreType.DMA((count + 1,)),
        ],
        compiler_params=pltpu.CompilerParams(vmem_limit_bytes=STREAM),
        cost_estimate=pl.CostEstimate(
            flops=2 * tokens * features * width,
            bytes_accessed=2 * features * width,
            transcendentals=0,
        ),
    )(heads, proj)


def norm_kernel(count, parts_ref, residual_ref, gain_ref, ids_ref, codes_ref, hidden_ref, rows_ref):
    size, width = residual_ref.shape
    hidden = residual_ref[...].astype(jnp.float32)
    attn = parts_ref[:size].astype(jnp.float32)
    for i in range(1, count):
        attn = attn + parts_ref[i * size : (i + 1) * size].astype(jnp.float32)
    hidden = hidden + attn
    hidden_ref[...] = hidden
    mean_square = jnp.mean(hidden * hidden, axis=-1, keepdims=True)
    normed = (hidden * lax.rsqrt(mean_square + 1e-06) * gain_ref[...]).astype(jnp.bfloat16)
    ids, codes = ids_ref[...], codes_ref[...]
    lane = lax.broadcasted_iota(jnp.int32, (size, LANES), 1)
    table = jnp.zeros((size, LANES), jnp.int32)
    for k in range(ids.shape[1]):
        code = codes[:, k : k + 1]
        table = table + jnp.where((lane == ids[:, k : k + 1]) | (lane == EXPERTS), code, 0)
    table = table.astype(jnp.float32).astype(jnp.bfloat16)
    for i in range(count):
        rows_ref[i * size : (i + 1) * size, :width] = normed
        rows_ref[i * size : (i + 1) * size, width:] = table


def normalize(parts, residual, gain, ids, codes, count):
    size, width = residual.shape
    return pl.pallas_call(
        functools.partial(norm_kernel, count),
        out_shape=[
            jax.ShapeDtypeStruct((size, width), jnp.float32),
            jax.ShapeDtypeStruct((count * size, width + LANES), jnp.bfloat16),
        ],
        in_specs=[vmem_spec()] * 5,
        out_specs=[vmem_spec()] * 2,
        compiler_params=pltpu.CompilerParams(vmem_limit_bytes=GRANT),
        cost_estimate=pl.CostEstimate(
            flops=20 * size * width, bytes_accessed=6 * count * size * width, transcendentals=size
        ),
    )(parts, residual, gain, ids, codes)


def swap_over_tensor(value):
    return lax.all_to_all(value, "tensor", split_axis=0, concat_axis=0, tiled=True)


def shift(value, turn, step):
    pairs = []
    for half in range(lax.axis_size("dp")):
        for row in range(SIDE):
            for col in range(SIDE):
                if (half + turn) % 2:
                    to_row, to_col = (row + step) % SIDE, col
                else:
                    to_row, to_col = row, (col + step) % SIDE
                base = half * SIDE * SIDE
                pairs.append((base + row * SIDE + col, base + to_row * SIDE + to_col))
    return lax.ppermute(value, ("dp", "expert"), pairs)


def add(*values):
    total = values[0].astype(jnp.float32)
    for value in values[1:]:
        total = total + value.astype(jnp.float32)
    return total


def tie(values, others):
    tied = lax.optimization_barrier((*values, *others))
    return tied[: len(values)], tied[len(values) :]


def packing(tail, expert, slots):
    rows = tail.shape[0]
    named = jnp.where(tail.astype(jnp.float32) > 0.0, 1.0, 0.0).astype(jnp.bfloat16)
    square = (rows, rows)
    below = lax.broadcasted_iota(jnp.int32, square, 0) > lax.broadcasted_iota(jnp.int32, square, 1)
    before = jnp.dot(
        jnp.where(below, 1.0, 0.0).astype(jnp.bfloat16), named, preferred_element_type=jnp.float32
    ).astype(jnp.bfloat16)
    lane = lax.broadcasted_iota(jnp.int32, (8, tail.shape[1]), 1)
    pick = jnp.where(lane == expert, 1.0, 0.0).astype(jnp.bfloat16)
    both_last = (((1,), (1,)), ((), ()))
    is_named = lax.dot_general(pick, named, both_last, preferred_element_type=jnp.float32)
    place = lax.dot_general(pick, before, both_last, preferred_element_type=jnp.float32)
    slot = lax.broadcasted_iota(jnp.int32, (slots, rows), 0).astype(jnp.float32)
    fills = (slot == place[:1]) & (is_named[:1] > 0.5)
    return jnp.where(fills, 1.0, 0.0).astype(jnp.bfloat16)


def beside(me_ref, dp_ref):
    row, col = me_ref[0] // SIDE, me_ref[0] % SIDE
    first = dp_ref[0] == 0
    ahead = jnp.where(first, (row + 1) % SIDE * SIDE + col, row * SIDE + (col + 1) % SIDE)
    back_row, back_col = (row + SIDE - 1) % SIDE, (col + SIDE - 1) % SIDE
    return ahead, jnp.where(first, back_row * SIDE + col, row * SIDE + back_col)


def chosen(hot, rows):
    return jnp.dot(hot, rows, preferred_element_type=jnp.float32).astype(jnp.bfloat16)


def unpacked(hot_ref, value):
    over_slots = (((0,), (0,)), ((), ()))
    return lax.dot_general(hot_ref[...], value, over_slots, preferred_element_type=jnp.float32)


def line_kernel(me_ref, dp_ref, _, low_ref, *refs):
    *highs, line_ref, to_ahead_ref, to_behind_ref, ahead_hot_ref, behind_hot_ref = refs
    slots, half = ahead_hot_ref.shape
    ahead, behind = beside(me_ref, dp_ref)
    tail = low_ref.shape[1] - LANES
    low, high = low_ref[...], jnp.concatenate([ref[...] for ref in highs])
    ahead_hot = packing(high[:, tail:], ahead, slots)
    behind_hot = packing(low[:, tail:], behind, slots)
    line_ref[:half, :] = low
    line_ref[half:, :] = high
    to_ahead_ref[:half, :] = low
    to_ahead_ref[half:, :] = chosen(ahead_hot, high)
    to_behind_ref[:slots, :] = chosen(behind_hot, low)
    to_behind_ref[slots:, :] = high
    ahead_hot_ref[...] = ahead_hot
    behind_hot_ref[...] = behind_hot


def make_line(me, dp, after, low, *highs):
    half, width = low.shape
    slots = half // TOP_TOKENS * CAP
    smem = pl.BlockSpec(memory_space=pltpu.SMEM)
    shapes = [(2 * half, width)] + [(half + slots, width)] * 2 + [(slots, half)] * 2
    return pl.pallas_call(
        line_kernel,
        out_shape=[jax.ShapeDtypeStruct(shape, jnp.bfloat16) for shape in shapes],
        in_specs=[smem] * 2 + [pl.BlockSpec(memory_space=pl.ANY)] + [vmem_spec()] * (1 + len(highs)),
        out_specs=[vmem_spec()] * 5,
        compiler_params=pltpu.CompilerParams(vmem_limit_bytes=GRANT),
        cost_estimate=pl.CostEstimate(
            flops=4 * half * slots * width, bytes_accessed=12 * half * width, transcendentals=0
        ),
    )(me, dp, after, low, *highs)


def pack_kernel(
    me_ref, dp_ref, _, back_ref, front_ref, low_ref, high_ref, low_hot_ref, high_hot_ref
):
    slots, half = low_hot_ref.shape
    ahead, behind = beside(me_ref, dp_ref)
    tail = low_ref.shape[1] - LANES
    low_hot = packing(back_ref[:half, tail:], ahead, slots)
    high_hot = packing(front_ref[slots:, tail:], behind, slots)
    low_hot_ref[...] = low_hot
    high_hot_ref[...] = high_hot
    low_ref[...] = chosen(low_hot, back_ref[:half, :])
    high_ref[...] = chosen(high_hot, front_ref[slots:, :])


def pack(me, dp, half, after, back, front):
    rows, width = back.shape
    slots = rows - half
    smem = pl.BlockSpec(memory_space=pltpu.SMEM)
    return pl.pallas_call(
        pack_kernel,
        out_shape=[jax.ShapeDtypeStruct((slots, width), jnp.bfloat16)] * 2
        + [jax.ShapeDtypeStruct((slots, half), jnp.bfloat16)] * 2,
        in_specs=[smem] * 2 + [pl.BlockSpec(memory_space=pl.ANY)] + [vmem_spec()] * 2,
        out_specs=[vmem_spec()] * 4,
        compiler_params=pltpu.CompilerParams(vmem_limit_bytes=GRANT),
        cost_estimate=pl.CostEstimate(
            flops=4 * half * slots * width, bytes_accessed=4 * rows * width, transcendentals=0
        ),
    )(me, dp, after, back, front)


def join_kernel(
    _, back_ref, front_ref, low_ref, high_ref, low_hot_ref, high_hot_ref, to_front_ref, to_back_ref
):
    slots, half = low_hot_ref.shape
    low = back_ref[:half, :].astype(jnp.float32) + unpacked(low_hot_ref, low_ref[...])
    high = front_ref[slots:, :].astype(jnp.float32) + unpacked(high_hot_ref, high_ref[...])
    to_back_ref[:half, :] = low.astype(jnp.bfloat16)
    to_back_ref[half:, :] = back_ref[half:, :]
    to_front_ref[:slots, :] = front_ref[:slots, :]
    to_front_ref[slots:, :] = high.astype(jnp.bfloat16)


def join(after, back, front, low, high, low_hot, high_hot):
    rows, width = back.shape
    return pl.pallas_call(
        join_kernel,
        out_shape=[jax.ShapeDtypeStruct((rows, width), jnp.bfloat16)] * 2,
        in_specs=[pl.BlockSpec(memory_space=pl.ANY)] + [vmem_spec()] * 6,
        out_specs=[vmem_spec()] * 2,
        compiler_params=pltpu.CompilerParams(vmem_limit_bytes=GRANT),
        cost_estimate=pl.CostEstimate(
            flops=2 * rows * low.shape[0] * width, bytes_accessed=10 * rows * width, transcendentals=0
        ),
    )(after, back, front, low, high, low_hot, high_hot)


def total_kernel(own_ref, back_ref, front_ref, ahead_hot_ref, behind_hot_ref, low_ref, *highs):
    slots, half = ahead_hot_ref.shape
    low = add(own_ref[:half, :], front_ref[:half, :]) + unpacked(behind_hot_ref, back_ref[:slots, :])
    low_ref[...] = low.astype(jnp.bfloat16)
    high = add(own_ref[half:, :], back_ref[slots:, :]) + unpacked(ahead_hot_ref, front_ref[half:, :])
    high = high.astype(jnp.bfloat16)
    size = highs[0].shape[0]
    for i, out in enumerate(highs):
        out[...] = high[i * size : (i + 1) * size]


def total(own, got, hots, sizes):
    rows, width = own.shape
    return pl.pallas_call(
        total_kernel,
        out_shape=[jax.ShapeDtypeStruct((size, width), jnp.bfloat16) for size in sizes],
        in_specs=[vmem_spec()] * 5,
        out_specs=[vmem_spec()] * len(sizes),
        compiler_params=pltpu.CompilerParams(vmem_limit_bytes=GRANT),
        cost_estimate=pl.CostEstimate(
            flops=2 * rows * width, bytes_accessed=8 * rows * width, transcendentals=0
        ),
    )(own, *got, *hots)


def join_last_kernel(front_ref, back_ref, up_ref, down_ref, to_front_ref, to_back_ref):
    half = up_ref.shape[0]
    to_front_ref[:half, :] = add(front_ref[:half, :], up_ref[...]).astype(jnp.bfloat16)
    to_front_ref[half:, :] = front_ref[half:, :]
    to_back_ref[:half, :] = back_ref[:half, :]
    to_back_ref[half:, :] = add(back_ref[half:, :], down_ref[...]).astype(jnp.bfloat16)


def join_last(front, back, up, down):
    rows, width = front.shape
    return pl.pallas_call(
        join_last_kernel,
        out_shape=[jax.ShapeDtypeStruct((rows, width), jnp.bfloat16)] * 2,
        in_specs=[vmem_spec()] * 4,
        out_specs=[vmem_spec()] * 2,
        compiler_params=pltpu.CompilerParams(vmem_limit_bytes=GRANT),
        cost_estimate=pl.CostEstimate(
            flops=rows * width, bytes_accessed=10 * rows * width, transcendentals=0
        ),
    )(front, back, up, down)


def expert_kernel(count, me_ref, _, *refs):
    blocks, (gate_ref, up_ref, down_ref), outs = refs[:count], refs[count : count + 3], refs[count + 3 :]
    width = gate_ref.shape[1]
    x = jnp.concatenate([block[:, :width] for block in blocks])
    tail = jnp.concatenate([block[:, width:] for block in blocks]).astype(jnp.float32)
    lane = lax.broadcasted_iota(jnp.int32, tail.shape, 1)
    code = jnp.sum(jnp.where(lane == me_ref[0], tail, 0.0), axis=1, keepdims=True)
    total = jnp.sum(jnp.where(lane == EXPERTS, tail, 0.0), axis=1, keepdims=True)
    both_last = (((1,), (1,)), ((), ()))
    gate_value = lax.dot_general(x, gate_ref[...], both_last, preferred_element_type=jnp.float32)
    up_value = lax.dot_general(x, up_ref[...], both_last, preferred_element_type=jnp.float32)
    activated = (jax.nn.silu(gate_value) * up_value).astype(jnp.bfloat16)
    scale = code / jnp.maximum(total, 1.0)
    size = outs[0].shape[0]
    for start in range(0, width, CHUNK):
        down = jnp.dot(
            activated, down_ref[:, start : start + CHUNK], preferred_element_type=jnp.float32
        )
        result = (down * scale).astype(jnp.bfloat16)
        for i, out in enumerate(outs):
            out[:, start : start + CHUNK] = result[i * size : (i + 1) * size]


def run_expert(me, after, blocks, w_gate, w_up, w_down):
    count, size = len(blocks), blocks[0].shape[0]
    units, width = w_gate.shape
    vmem = pl.BlockSpec(memory_space=pltpu.VMEM)
    return pl.pallas_call(
        functools.partial(expert_kernel, count),
        out_shape=[jax.ShapeDtypeStruct((size, width), jnp.bfloat16)] * count,
        in_specs=[pl.BlockSpec(memory_space=pltpu.SMEM), pl.BlockSpec(memory_space=pl.ANY)]
        + [vmem] * (count + 3),
        out_specs=[vmem] * count,
        compiler_params=pltpu.CompilerParams(vmem_limit_bytes=GRANT),
        cost_estimate=pl.CostEstimate(
            flops=6 * count * size * units * width,
            bytes_accessed=4 * count * size * width + 6 * units * width,
            transcendentals=count * size * units,
        ),
    )(me, after, *blocks, w_gate, w_up, w_down)


def on_device(
    attn_heads, out_proj, residual, norm_gain, expert_ids, weight_codes, w_gate, w_up, w_down
):
    tensor_count = lax.axis_size("tensor")
    who = jnp.reshape(lax.axis_index("expert"), (1,)).astype(jnp.int32)
    side = jnp.reshape(lax.axis_index("dp"), (1,)).astype(jnp.int32)
    (heads,), (who, side) = tie((attn_heads[0],), (who, side))
    partial = project(heads, out_proj)
    hidden, rows = normalize(
        swap_over_tensor(partial),
        residual[0],
        norm_gain[None],
        expert_ids[0],
        weight_codes[0],
        tensor_count,
    )
    group = swap_over_tensor(rows)
    tokens, model_width = partial.shape

    weights = (w_gate[0], w_up[0], w_down[0])

    def experts(*blocks, after):
        return run_expert(who, after, blocks, *weights)

    def both(ahead, behind, turn):
        return shift(ahead, turn, 1), shift(behind, turn, -1)

    half = tokens // 2
    back, front = both(group, group, 0)
    first, *first_sent, first_ahead, first_behind = make_line(who, side, front, group, back)
    first_near = both(*first_sent, 1)
    far = both(back[:half], front[half:], 0)
    first_own = experts(first, after=back)
    second, *second_sent, second_ahead, second_behind = make_line(
        who, side, first_own[0], front, *far
    )
    second_near = both(*second_sent, 1)
    first_near_out = experts(*first_near, after=first_own[0])
    second_own = experts(second, after=first_near_out[0])
    low, high, *first_hot = pack(who, side, tokens, second_own[0], *first_near)
    first_far = both(low, high, 1)
    second_near, first_near_out = tie(second_near, first_near_out)
    low, high, *second_hot = pack(who, side, tokens, low, *second_near)
    second_far = both(low, high, 1)
    first_far_low, first_far_high = experts(*first_far, after=high)
    first_down = both(first_far_high, first_far_low, 1)[::-1]
    second_far_low, second_far_high = experts(*second_far, after=first_far_low)
    second_down = both(second_far_high, second_far_low, 1)[::-1]
    second_near_out = experts(*second_near, after=second_far_low)
    first_down, second_down = tie(first_down, second_down)
    second_send = join(second_near_out[0], *second_near_out, *second_down, *second_hot)
    first_send = join(second_send[0], *first_near_out, *first_down, *first_hot)
    first_got = both(*first_send, 1)
    second_got = both(*second_send, 1)
    own, back = total(first_own[0], first_got, (first_ahead, first_behind), (tokens, tokens))
    hots = (second_ahead, second_behind)
    front, low, high = total(second_own[0], second_got, hots, (tokens, half, half))
    got = both(*join_last(front, back, *both(low, high, 0)), 0)
    mixed = add(own, *got).astype(jnp.bfloat16)
    parts = swap_over_tensor(mixed).reshape(tensor_count, -1, model_width)
    layer_out = (hidden + jnp.sum(parts.astype(jnp.float32), axis=0)).astype(jnp.bfloat16)
    return layer_out[None]


def solution(mesh):
    return jax.shard_map(
        on_device,
        mesh=mesh,
        in_specs=(
            P(("dp", "expert"), None, "tensor"),
            P("tensor", None),
            P(("dp", "expert"), "tensor", None),
            P(),
            P(("dp", "expert"), "tensor", None),
            P(("dp", "expert"), "tensor", None),
            P("expert", "tensor", None),
            P("expert", "tensor", None),
            P("expert", "tensor", None),
        ),
        out_specs=P(("dp", "expert"), "tensor", None),
        check_vma=False,
    )
```

```python
import functools

import jax
import jax.numpy as jnp
from jax import lax
from jax.experimental import pallas as pl
from jax.experimental.pallas import tpu as pltpu
from jax.sharding import PartitionSpec as P

EXPERTS = 16
TOP_TOKENS, CAP = 8, 6
SIDE = 4
LANES = 128
CHUNK = 1024
STRIPE = 1024
GRANT = 8 << 20
STREAM = 62 << 20


def vmem_spec():
    return pl.BlockSpec(memory_space=pltpu.VMEM)


def project_kernel(heads_hbm, proj_hbm, out_ref, heads_ref, proj_ref, sems):
    count, _, size = proj_ref.shape
    copies = [pltpu.make_async_copy(heads_hbm, heads_ref, sems.at[count])]
    for i in range(count):
        columns = pl.ds(i * size, size)
        copies.append(
            pltpu.make_async_copy(proj_hbm.at[:, columns], proj_ref.at[i], sems.at[i])
        )
    for copy in copies:
        copy.start()
    copies[0].wait()
    heads = heads_ref[...]
    for i in range(count):
        copies[i + 1].wait()
        out_ref[:, i * size : (i + 1) * size] = jnp.dot(
            heads, proj_ref[i], preferred_element_type=jnp.float32
        ).astype(jnp.bfloat16)


def project(heads, proj):
    tokens, features = heads.shape
    width = proj.shape[1]
    count = width // STRIPE
    return pl.pallas_call(
        project_kernel,
        out_shape=jax.ShapeDtypeStruct((tokens, width), jnp.bfloat16),
        in_specs=[pl.BlockSpec(memory_space=pl.ANY)] * 2,
        out_specs=vmem_spec(),
        scratch_shapes=[
            pltpu.VMEM((tokens, features), jnp.bfloat16),
            pltpu.VMEM((count, features, STRIPE), jnp.bfloat16),
            pltpu.SemaphoreType.DMA((count + 1,)),
        ],
        compiler_params=pltpu.CompilerParams(vmem_limit_bytes=STREAM),
        cost_estimate=pl.CostEstimate(
            flops=2 * tokens * features * width,
            bytes_accessed=2 * features * width,
            transcendentals=0,
        ),
    )(heads, proj)


def norm_kernel(count, parts_ref, residual_ref, gain_ref, ids_ref, codes_ref, hidden_ref, rows_ref):
    size, width = residual_ref.shape
    hidden = residual_ref[...].astype(jnp.float32)
    attn = parts_ref[:size].astype(jnp.float32)
    for i in range(1, count):
        attn = attn + parts_ref[i * size : (i + 1) * size].astype(jnp.float32)
    hidden = hidden + attn
    hidden_ref[...] = hidden
    mean_square = jnp.mean(hidden * hidden, axis=-1, keepdims=True)
    normed = (hidden * lax.rsqrt(mean_square + 1e-06) * gain_ref[...]).astype(jnp.bfloat16)
    ids, codes = ids_ref[...], codes_ref[...]
    lane = lax.broadcasted_iota(jnp.int32, (size, LANES), 1)
    table = jnp.zeros((size, LANES), jnp.int32)
    for k in range(ids.shape[1]):
        code = codes[:, k : k + 1]
        table = table + jnp.where((lane == ids[:, k : k + 1]) | (lane == EXPERTS), code, 0)
    table = table.astype(jnp.float32).astype(jnp.bfloat16)
    for i in range(count):
        rows_ref[i * size : (i + 1) * size, :width] = normed
        rows_ref[i * size : (i + 1) * size, width:] = table


def normalize(parts, residual, gain, ids, codes, count):
    size, width = residual.shape
    return pl.pallas_call(
        functools.partial(norm_kernel, count),
        out_shape=[
            jax.ShapeDtypeStruct((size, width), jnp.float32),
            jax.ShapeDtypeStruct((count * size, width + LANES), jnp.bfloat16),
        ],
        in_specs=[vmem_spec()] * 5,
        out_specs=[vmem_spec()] * 2,
        compiler_params=pltpu.CompilerParams(vmem_limit_bytes=GRANT),
        cost_estimate=pl.CostEstimate(
            flops=20 * size * width, bytes_accessed=6 * count * size * width, transcendentals=size
        ),
    )(parts, residual, gain, ids, codes)


def swap_over_tensor(value):
    return lax.all_to_all(value, "tensor", split_axis=0, concat_axis=0, tiled=True)


def shift(value, turn, step):
    pairs = []
    for half in range(lax.axis_size("dp")):
        for row in range(SIDE):
            for col in range(SIDE):
                if (half + turn) % 2:
                    to_row, to_col = (row + step) % SIDE, col
                else:
                    to_row, to_col = row, (col + step) % SIDE
                base = half * SIDE * SIDE
                pairs.append((base + row * SIDE + col, base + to_row * SIDE + to_col))
    return lax.ppermute(value, ("dp", "expert"), pairs)


def add(*values):
    total = values[0].astype(jnp.float32)
    for value in values[1:]:
        total = total + value.astype(jnp.float32)
    return total


def tie(values, others):
    tied = lax.optimization_barrier((*values, *others))
    return tied[: len(values)], tied[len(values) :]


def packing(tail, expert, slots):
    rows = tail.shape[0]
    named = jnp.where(tail.astype(jnp.float32) > 0.0, 1.0, 0.0).astype(jnp.bfloat16)
    square = (rows, rows)
    below = lax.broadcasted_iota(jnp.int32, square, 0) > lax.broadcasted_iota(jnp.int32, square, 1)
    before = jnp.dot(
        jnp.where(below, 1.0, 0.0).astype(jnp.bfloat16), named, preferred_element_type=jnp.float32
    ).astype(jnp.bfloat16)
    lane = lax.broadcasted_iota(jnp.int32, (8, tail.shape[1]), 1)
    pick = jnp.where(lane == expert, 1.0, 0.0).astype(jnp.bfloat16)
    both_last = (((1,), (1,)), ((), ()))
    is_named = lax.dot_general(pick, named, both_last, preferred_element_type=jnp.float32)
    place = lax.dot_general(pick, before, both_last, preferred_element_type=jnp.float32)
    slot = lax.broadcasted_iota(jnp.int32, (slots, rows), 0).astype(jnp.float32)
    fills = (slot == place[:1]) & (is_named[:1] > 0.5)
    return jnp.where(fills, 1.0, 0.0).astype(jnp.bfloat16)


def beside(me_ref, dp_ref):
    row, col = me_ref[0] // SIDE, me_ref[0] % SIDE
    first = dp_ref[0] == 0
    ahead = jnp.where(first, (row + 1) % SIDE * SIDE + col, row * SIDE + (col + 1) % SIDE)
    back_row, back_col = (row + SIDE - 1) % SIDE, (col + SIDE - 1) % SIDE
    return ahead, jnp.where(first, back_row * SIDE + col, row * SIDE + back_col)


def chosen(hot, rows):
    return jnp.dot(hot, rows, preferred_element_type=jnp.float32).astype(jnp.bfloat16)


def unpacked(hot_ref, value):
    over_slots = (((0,), (0,)), ((), ()))
    return lax.dot_general(hot_ref[...], value, over_slots, preferred_element_type=jnp.float32)


def line_kernel(me_ref, dp_ref, _, low_ref, *refs):
    *highs, line_ref, to_ahead_ref, to_behind_ref, ahead_hot_ref, behind_hot_ref = refs
    slots, half = ahead_hot_ref.shape
    ahead, behind = beside(me_ref, dp_ref)
    tail = low_ref.shape[1] - LANES
    low, high = low_ref[...], jnp.concatenate([ref[...] for ref in highs])
    ahead_hot = packing(high[:, tail:], ahead, slots)
    behind_hot = packing(low[:, tail:], behind, slots)
    line_ref[:half, :] = low
    line_ref[half:, :] = high
    to_ahead_ref[:half, :] = low
    to_ahead_ref[half:, :] = chosen(ahead_hot, high)
    to_behind_ref[:slots, :] = chosen(behind_hot, low)
    to_behind_ref[slots:, :] = high
    ahead_hot_ref[...] = ahead_hot
    behind_hot_ref[...] = behind_hot


def make_line(me, dp, after, low, *highs):
    half, width = low.shape
    slots = half // TOP_TOKENS * CAP
    smem = pl.BlockSpec(memory_space=pltpu.SMEM)
    shapes = [(2 * half, width)] + [(half + slots, width)] * 2 + [(slots, half)] * 2
    return pl.pallas_call(
        line_kernel,
        out_shape=[jax.ShapeDtypeStruct(shape, jnp.bfloat16) for shape in shapes],
        in_specs=[smem] * 2 + [pl.BlockSpec(memory_space=pl.ANY)] + [vmem_spec()] * (1 + len(highs)),
        out_specs=[vmem_spec()] * 5,
        compiler_params=pltpu.CompilerParams(vmem_limit_bytes=GRANT),
        cost_estimate=pl.CostEstimate(
            flops=4 * half * slots * width, bytes_accessed=12 * half * width, transcendentals=0
        ),
    )(me, dp, after, low, *highs)


def pack_kernel(
    me_ref, dp_ref, _, back_ref, front_ref, low_ref, high_ref, low_hot_ref, high_hot_ref
):
    slots, half = low_hot_ref.shape
    ahead, behind = beside(me_ref, dp_ref)
    tail = low_ref.shape[1] - LANES
    low_hot = packing(back_ref[:half, tail:], ahead, slots)
    high_hot = packing(front_ref[slots:, tail:], behind, slots)
    low_hot_ref[...] = low_hot
    high_hot_ref[...] = high_hot
    low_ref[...] = chosen(low_hot, back_ref[:half, :])
    high_ref[...] = chosen(high_hot, front_ref[slots:, :])


def pack(me, dp, half, after, back, front):
    rows, width = back.shape
    slots = rows - half
    smem = pl.BlockSpec(memory_space=pltpu.SMEM)
    return pl.pallas_call(
        pack_kernel,
        out_shape=[jax.ShapeDtypeStruct((slots, width), jnp.bfloat16)] * 2
        + [jax.ShapeDtypeStruct((slots, half), jnp.bfloat16)] * 2,
        in_specs=[smem] * 2 + [pl.BlockSpec(memory_space=pl.ANY)] + [vmem_spec()] * 2,
        out_specs=[vmem_spec()] * 4,
        compiler_params=pltpu.CompilerParams(vmem_limit_bytes=GRANT),
        cost_estimate=pl.CostEstimate(
            flops=4 * half * slots * width, bytes_accessed=4 * rows * width, transcendentals=0
        ),
    )(me, dp, after, back, front)


def join_kernel(
    _, back_ref, front_ref, low_ref, high_ref, low_hot_ref, high_hot_ref, to_front_ref, to_back_ref
):
    slots, half = low_hot_ref.shape
    low = back_ref[:half, :].astype(jnp.float32) + unpacked(low_hot_ref, low_ref[...])
    high = front_ref[slots:, :].astype(jnp.float32) + unpacked(high_hot_ref, high_ref[...])
    to_back_ref[:half, :] = low.astype(jnp.bfloat16)
    to_back_ref[half:, :] = back_ref[half:, :]
    to_front_ref[:slots, :] = front_ref[:slots, :]
    to_front_ref[slots:, :] = high.astype(jnp.bfloat16)


def join(after, back, front, low, high, low_hot, high_hot):
    rows, width = back.shape
    return pl.pallas_call(
        join_kernel,
        out_shape=[jax.ShapeDtypeStruct((rows, width), jnp.bfloat16)] * 2,
        in_specs=[pl.BlockSpec(memory_space=pl.ANY)] + [vmem_spec()] * 6,
        out_specs=[vmem_spec()] * 2,
        compiler_params=pltpu.CompilerParams(vmem_limit_bytes=GRANT),
        cost_estimate=pl.CostEstimate(
            flops=2 * rows * low.shape[0] * width, bytes_accessed=10 * rows * width, transcendentals=0
        ),
    )(after, back, front, low, high, low_hot, high_hot)


def total_kernel(own_ref, back_ref, front_ref, ahead_hot_ref, behind_hot_ref, low_ref, *highs):
    slots, half = ahead_hot_ref.shape
    low = add(own_ref[:half, :], front_ref[:half, :]) + unpacked(behind_hot_ref, back_ref[:slots, :])
    low_ref[...] = low.astype(jnp.bfloat16)
    high = add(own_ref[half:, :], back_ref[slots:, :]) + unpacked(ahead_hot_ref, front_ref[half:, :])
    high = high.astype(jnp.bfloat16)
    size = highs[0].shape[0]
    for i, out in enumerate(highs):
        out[...] = high[i * size : (i + 1) * size]


def total(own, got, hots, sizes):
    rows, width = own.shape
    return pl.pallas_call(
        total_kernel,
        out_shape=[jax.ShapeDtypeStruct((size, width), jnp.bfloat16) for size in sizes],
        in_specs=[vmem_spec()] * 5,
        out_specs=[vmem_spec()] * len(sizes),
        compiler_params=pltpu.CompilerParams(vmem_limit_bytes=GRANT),
        cost_estimate=pl.CostEstimate(
            flops=2 * rows * width, bytes_accessed=8 * rows * width, transcendentals=0
        ),
    )(own, *got, *hots)


def join_last_kernel(front_ref, back_ref, up_ref, down_ref, to_front_ref, to_back_ref):
    half = up_ref.shape[0]
    to_front_ref[:half, :] = add(front_ref[:half, :], up_ref[...]).astype(jnp.bfloat16)
    to_front_ref[half:, :] = front_ref[half:, :]
    to_back_ref[:half, :] = back_ref[:half, :]
    to_back_ref[half:, :] = add(back_ref[half:, :], down_ref[...]).astype(jnp.bfloat16)


def join_last(front, back, up, down):
    rows, width = front.shape
    return pl.pallas_call(
        join_last_kernel,
        out_shape=[jax.ShapeDtypeStruct((rows, width), jnp.bfloat16)] * 2,
        in_specs=[vmem_spec()] * 4,
        out_specs=[vmem_spec()] * 2,
        compiler_params=pltpu.CompilerParams(vmem_limit_bytes=GRANT),
        cost_estimate=pl.CostEstimate(
            flops=rows * width, bytes_accessed=10 * rows * width, transcendentals=0
        ),
    )(front, back, up, down)


def expert_kernel(count, me_ref, _, *refs):
    blocks, (gate_ref, up_ref, down_ref), outs = refs[:count], refs[count : count + 3], refs[count + 3 :]
    width = gate_ref.shape[1]
    x = jnp.concatenate([block[:, :width] for block in blocks])
    tail = jnp.concatenate([block[:, width:] for block in blocks]).astype(jnp.float32)
    lane = lax.broadcasted_iota(jnp.int32, tail.shape, 1)
    code = jnp.sum(jnp.where(lane == me_ref[0], tail, 0.0), axis=1, keepdims=True)
    total = jnp.sum(jnp.where(lane == EXPERTS, tail, 0.0), axis=1, keepdims=True)
    both_last = (((1,), (1,)), ((), ()))
    gate_value = lax.dot_general(x, gate_ref[...], both_last, preferred_element_type=jnp.float32)
    up_value = lax.dot_general(x, up_ref[...], both_last, preferred_element_type=jnp.float32)
    activated = (jax.nn.silu(gate_value) * up_value).astype(jnp.bfloat16)
    scale = code / jnp.maximum(total, 1.0)
    size = outs[0].shape[0]
    for start in range(0, width, CHUNK):
        down = jnp.dot(
            activated, down_ref[:, start : start + CHUNK], preferred_element_type=jnp.float32
        )
        result = (down * scale).astype(jnp.bfloat16)
        for i, out in enumerate(outs):
            out[:, start : start + CHUNK] = result[i * size : (i + 1) * size]


def run_expert(me, after, blocks, w_gate, w_up, w_down):
    count, size = len(blocks), blocks[0].shape[0]
    units, width = w_gate.shape
    vmem = pl.BlockSpec(memory_space=pltpu.VMEM)
    return pl.pallas_call(
        functools.partial(expert_kernel, count),
        out_shape=[jax.ShapeDtypeStruct((size, width), jnp.bfloat16)] * count,
        in_specs=[pl.BlockSpec(memory_space=pltpu.SMEM), pl.BlockSpec(memory_space=pl.ANY)]
        + [vmem] * (count + 3),
        out_specs=[vmem] * count,
        compiler_params=pltpu.CompilerParams(vmem_limit_bytes=GRANT),
        cost_estimate=pl.CostEstimate(
            flops=6 * count * size * units * width,
            bytes_accessed=4 * count * size * width + 6 * units * width,
            transcendentals=count * size * units,
        ),
    )(me, after, *blocks, w_gate, w_up, w_down)


def on_device(
    attn_heads, out_proj, residual, norm_gain, expert_ids, weight_codes, w_gate, w_up, w_down
):
    tensor_count = lax.axis_size("tensor")
    who = jnp.reshape(lax.axis_index("expert"), (1,)).astype(jnp.int32)
    side = jnp.reshape(lax.axis_index("dp"), (1,)).astype(jnp.int32)
    (heads,), (who, side) = tie((attn_heads[0],), (who, side))
    partial = project(heads, out_proj)
    hidden, rows = normalize(
        swap_over_tensor(partial),
        residual[0],
        norm_gain[None],
        expert_ids[0],
        weight_codes[0],
        tensor_count,
    )
    group = swap_over_tensor(rows)
    tokens, model_width = partial.shape

    weights = (w_gate[0], w_up[0], w_down[0])

    def experts(*blocks, after):
        return run_expert(who, after, blocks, *weights)

    def both(ahead, behind, turn):
        return shift(ahead, turn, 1), shift(behind, turn, -1)

    half = tokens // 2
    back, front = both(group, group, 0)
    first, *first_sent, first_ahead, first_behind = make_line(who, side, front, group, back)
    first_near = both(*first_sent, 1)
    far = both(back[:half], front[half:], 0)
    first_own = experts(first, after=back)
    second, *second_sent, second_ahead, second_behind = make_line(
        who, side, first_own[0], front, *far
    )
    second_near = both(*second_sent, 1)
    first_near_out = experts(*first_near, after=first_own[0])
    second_own = experts(second, after=first_near_out[0])
    low, high, *first_hot = pack(who, side, tokens, second_own[0], *first_near)
    first_far = both(low, high, 1)
    second_near, first_near_out = tie(second_near, first_near_out)
    low, high, *second_hot = pack(who, side, tokens, low, *second_near)
    second_far = both(low, high, 1)
    first_far_low, first_far_high = experts(*first_far, after=high)
    first_down = both(first_far_high, first_far_low, 1)[::-1]
    second_far_low, second_far_high = experts(*second_far, after=first_far_low)
    second_down = both(second_far_high, second_far_low, 1)[::-1]
    second_near_out = experts(*second_near, after=second_far_low)
    first_down, second_down = tie(first_down, second_down)
    first_send = join(second_near_out[0], *first_near_out, *first_down, *first_hot)
    second_send = join(first_send[1], *second_near_out, *second_down, *second_hot)
    first_got = both(*first_send, 1)
    second_got = both(*second_send, 1)
    own, back = total(first_own[0], first_got, (first_ahead, first_behind), (tokens, tokens))
    hots = (second_ahead, second_behind)
    front, low, high = total(second_own[0], second_got, hots, (tokens, half, half))
    got = both(*join_last(front, back, *both(low, high, 0)), 0)
    mixed = add(own, *got).astype(jnp.bfloat16)
    parts = swap_over_tensor(mixed).reshape(tensor_count, -1, model_width)
    layer_out = (hidden + jnp.sum(parts.astype(jnp.float32), axis=0)).astype(jnp.bfloat16)
    return layer_out[None]


def solution(mesh):
    return jax.shard_map(
        on_device,
        mesh=mesh,
        in_specs=(
            P(("dp", "expert"), None, "tensor"),
            P("tensor", None),
            P(("dp", "expert"), "tensor", None),
            P(),
            P(("dp", "expert"), "tensor", None),
            P(("dp", "expert"), "tensor", None),
            P("expert", "tensor", None),
            P("expert", "tensor", None),
            P("expert", "tensor", None),
        ),
        out_specs=P(("dp", "expert"), "tensor", None),
        check_vma=False,
    )
```
